32 devices in a mesh: pat: 8 (over y, x, core), feat: 4 (over z).
Axes of the slice: x: 2, y: 2, z: 4, core: 2. Of those that a mesh axis runs over, the one named last changes fastest.
Arguments:
- visits: bfloat16 [32768, 8192], P('pat', 'feat'), may hold values from -1.5 to 1.5
- counts: int32 [64], P('pat'), may hold values from 128 to 512, as said below
- patient_weight: float32 [64, 128], P('pat'), may hold values from 0.5 to 2
- phenotype_core: float32 [128, 128], replicated, may hold values from -0.5 to 0.5
- feature_factor: bfloat16 [8192, 128], P('feat'), may hold values from -0.0625 to 0.0625
- static_data: bfloat16 [64, 4096], P('pat', 'feat'), may hold values from -6 to 6
- static_factor: bfloat16 [4096, 128], P('feat'), may hold values from -0.09375 to 0.09375
Outputs:
- core_new: float32 [128, 128], replicated
- feature_new: float32 [8192, 128], P('feat')
- patient_new: float32 [64, 128], P('pat')
- static_new: float32 [4096, 128], P('feat')
The draws below stay inside these ranges and needn't reach their ends.
Inputs may be any that keep to these rules, and one draw needn't show every extreme that they name: `counts`: some patient of the last index of pat has exactly 512 visits.
All inputs are finite; a program needn't handle non-finite values.
Results may differ from the reference program's by a relative error of at most 0.0035.
Values may be sent and summed in bfloat16 or wider, within the bound.
A program may use at most 64 MiB of HBM per device.

```python
import math
import jax
import jax.numpy as jnp
from jax import lax

J = 8192
R = 128
P_SIZE = 4096
MAXV = 512
BLK = 128
SUB = 32
NS_STEPS = 8
PAT_DEV = 8
VIS_DEV = 4096
K = 64
VISITS = 32768
N_PAT = 8


def draw_counts(key, part):
    device_of = jnp.arange(K, dtype=jnp.int32) // PAT_DEV
    group_count = K // PAT_DEV
    upper_end = R + (MAXV - R) * (device_of + 1) // group_count
    drawn_counts = jax.random.randint(key, (K,), R, upper_end + 1, dtype=jnp.int32)
    full_spot = K - PAT_DEV + jax.random.randint(jax.random.fold_in(key, 7), (), 0, PAT_DEV, dtype=jnp.int32)
    return jnp.where(jnp.arange(K, dtype=jnp.int32) == full_spot, MAXV, drawn_counts).astype(jnp.int32)


def block_levels(own_key, dims, shards, least, top_value):
    level = 1.0
    for axis_at, blocks in shards:
        heights = jax.random.uniform(jax.random.fold_in(jax.random.fold_in(own_key, 6), axis_at), (blocks,), jnp.float32, least / len(shards), top_value / len(shards))
        level = level * jnp.repeat(jnp.exp(heights), dims[axis_at] // blocks).reshape((-1,) + (1,) * (len(dims) - 1 - axis_at))
    return level


def gaussian(stream_key, shape, spread, reach, cuts=(), held_as=jnp.bfloat16):
    values = jax.random.normal(stream_key, shape, jnp.float32) * spread
    if len(cuts) > 0:
        values = block_levels(stream_key, shape, cuts, -0.22, 0.18) * values
    return jnp.clip(values, min=-reach, max=reach).astype(held_as)


def setup_inputs(seed: int = 0) -> dict:
    arg_keys = jax.random.split(jax.random.key(seed), 8)
    visits = gaussian(arg_keys[0], (VISITS, J), 0.25, 1.5, ((0, 8), (1, 4)))
    counts = draw_counts(jax.random.fold_in(arg_keys[7], 71), 0)
    patient_weight = jnp.clip(jnp.exp(math.log(2.0) - 1.3862944 * jax.random.uniform(arg_keys[2], (K, R), jnp.float32) ** block_levels(arg_keys[2], (K, R), ((0, 8),), -0.2, 0.2)), 0.5, 2.0)
    phenotype_core = gaussian(arg_keys[3], (R, R), R ** -0.5, 0.5, (), jnp.float32)
    feature_factor = gaussian(arg_keys[4], (J, R), J ** -0.5, 0.0625, ((0, 4),))
    static_data = gaussian(arg_keys[5], (K, P_SIZE), 1.0, 6.0, ((0, 8), (1, 4)))
    static_factor = gaussian(arg_keys[6], (P_SIZE, R), P_SIZE ** -0.5, 0.09375, ((0, 4),))
    return {"visits": visits, "counts": counts, "patient_weight": patient_weight, "phenotype_core": phenotype_core, "feature_factor": feature_factor, "static_data": static_data, "static_factor": static_factor}


MU_RIDGE = 1.0

def layout(counts, rows, first):
    padded = (counts + BLK - 1) // BLK * BLK
    starts = jnp.cumsum(padded) - padded
    positions = first + jnp.arange(rows, dtype=jnp.int32)
    live = (positions[:, None] >= starts[None, :]) & (positions[:, None] < (starts + counts)[None, :])
    leading = positions[::SUB]
    member = (leading[:, None] >= starts[None, :]) & (leading[:, None] < (starts + padded)[None, :])
    return (live.astype(jnp.float32), member.astype(jnp.float32))

def contract_rows(left, right):
    return lax.dot_general(left, right, (((0,), (0,)), ((), ())), precision=lax.Precision.HIGHEST)

def core_field(projected, weight_rows, core):
    return lax.dot_general(projected * weight_rows, core, (((1,), (1,)), ((), ())), precision=lax.Precision.HIGHEST)

def block_grams(field, block_owner):
    pieces = field.reshape(-1, SUB, field.shape[1])
    grams = jnp.einsum('bvr,bvs->brs', pieces, pieces, precision=lax.Precision.HIGHEST)
    return jnp.einsum('bp,brs->prs', block_owner, grams, precision=lax.Precision.HIGHEST)

def batched(left, right):
    return jnp.einsum('nij,njk->nik', left, right, precision=lax.Precision.HIGHEST)

def polar_factor(grams):
    identity = jnp.eye(grams.shape[-1], dtype=jnp.float32)
    traces = jnp.trace(grams, axis1=1, axis2=2)
    moment = grams / traces[:, None, None]
    factor = identity[None] / jnp.sqrt(traces)[:, None, None]
    for iteration in range(NS_STEPS):
        correction = 1.5 * identity - 0.5 * moment
        factor = batched(factor, correction)
        moment = batched(batched(correction, moment), correction)
    return factor

def finish(field, projected, weight_rows, block_owner, row_owner, factor, core):
    rank = field.shape[1]
    block_factor = jnp.einsum('bp,prs->brs', block_owner, factor, precision=lax.Precision.HIGHEST)
    pieces = field.reshape(-1, SUB, rank)
    ortho = jnp.einsum('bvr,brs->bvs', pieces, block_factor, precision=lax.Precision.HIGHEST).reshape(-1, rank)
    mapped = jnp.dot(ortho, core, precision=lax.Precision.HIGHEST)
    patient_terms = contract_rows(row_owner, mapped * projected)
    core_terms = contract_rows(ortho, projected * weight_rows)
    update = (mapped * weight_rows).astype(jnp.bfloat16)
    return (patient_terms, core_terms, update)

def solve_right(rhs, matrix):
    lower = jnp.linalg.cholesky(matrix)
    return jax.scipy.linalg.cho_solve((lower, True), rhs.T).T

def reference(visits, counts, patient_weight, phenotype_core, feature_factor, static_data, static_factor):
    rows = VIS_DEV
    identity = jnp.eye(R, dtype=jnp.float32)
    features_wide = feature_factor.astype(jnp.float32)

    def per_group(carry, inputs):
        block, group_counts, group_weight = inputs
        block_wide = block.astype(jnp.float32)
        projected = jnp.dot(block_wide, features_wide, precision=lax.Precision.HIGHEST)
        row_owner, block_owner = layout(group_counts, rows, 0)
        weight_rows = jnp.dot(row_owner, group_weight, precision=lax.Precision.HIGHEST)
        field = core_field(projected, weight_rows, phenotype_core)
        factor = polar_factor(block_grams(field, block_owner))
        patient_terms, core_terms, update = finish(field, projected, weight_rows, block_owner, row_owner, factor, phenotype_core)
        feature_terms = contract_rows(block_wide, update.astype(jnp.float32))
        return ((carry[0] + feature_terms, carry[1] + core_terms), patient_terms)
    start_carry = (jnp.zeros((J, R), jnp.float32), jnp.zeros((R, R), jnp.float32))
    stacked = (visits.reshape(N_PAT, rows, J), counts.reshape(N_PAT, PAT_DEV), patient_weight.reshape(N_PAT, PAT_DEV, R))
    (feature_terms, core_terms), patient_terms = lax.scan(per_group, start_carry, stacked)
    patient_terms = patient_terms.reshape(K, R)
    coupled = jnp.dot(static_data.astype(jnp.float32), static_factor.astype(jnp.float32), preferred_element_type=jnp.float32)
    static_terms = contract_rows(static_data.astype(jnp.float32), patient_weight)
    core_gram = contract_rows(phenotype_core, phenotype_core)
    weight_gram = contract_rows(patient_weight, patient_weight)
    feature_gram = lax.dot_general(feature_factor.astype(jnp.float32), feature_factor.astype(jnp.float32), (((0,), (0,)), ((), ())), preferred_element_type=jnp.float32)
    static_gram = lax.dot_general(static_factor.astype(jnp.float32), static_factor.astype(jnp.float32), (((0,), (0,)), ((), ())), preferred_element_type=jnp.float32)
    core_new = solve_right(core_terms, feature_gram * weight_gram + MU_RIDGE * identity)
    feature_new = solve_right(feature_terms, core_gram * weight_gram + MU_RIDGE * identity)
    patient_new = solve_right(patient_terms + coupled, core_gram * feature_gram + static_gram + MU_RIDGE * identity)
    static_new = solve_right(static_terms, weight_gram + MU_RIDGE * identity)
    return (core_new, feature_new, patient_new, static_new)
```

```python
import functools

import jax
import jax.numpy as jnp
from jax import lax
from jax.experimental import pallas as pl
from jax.experimental.pallas import tpu as pltpu
from jax.sharding import PartitionSpec as P

BLK = 128
NS_STEPS = 8
MU_RIDGE = 1.0
MAXV = 512
LEVELS = 32766.0
F32 = jnp.float32
BF16 = jnp.bfloat16
MESH = pl.DeviceIdType.MESH

NN = (((1,), (0,)), ((), ()))
NT = (((1,), (1,)), ((), ()))
TN = (((0,), (0,)), ((), ()))


def dg(a, b, dims):
    return lax.dot_general(a, b, dims, preferred_element_type=F32)


def split(x):
    hi = x.astype(BF16)
    return hi, (x - hi.astype(F32)).astype(BF16)


def join(x):
    return jnp.concatenate(split(x), axis=1)


def twice(x):
    wide = join(x)
    return jnp.concatenate([wide, wide], axis=0)


def halves_sum(x):
    n = x.shape[1] // 2
    return x[:, :n] + x[:, n:]


def dot4(a, b):
    return halves_sum(dg(join(a), twice(b), NN))


def dot4_nt(a, b):
    hi, lo = split(b)
    rows = jnp.concatenate(
        [jnp.concatenate([hi, hi], axis=1), jnp.concatenate([lo, lo], axis=1)], axis=0
    )
    return halves_sum(dg(join(a), rows, NT))


def dot4_tn(a, b):
    return halves_sum(dg(jnp.concatenate(split(a), axis=0), twice(b), TN))


def exact(a, b, dims=NN):
    return lax.dot_general(
        a, b, dims, precision=lax.Precision.HIGHEST, preferred_element_type=F32
    )


def solve(rhs, matrix, inverse):
    guess = dot4(rhs, inverse)
    return guess + dot4(rhs - exact(guess, matrix), inverse)


def kernel(
    n_pat, n_feat, chunks, tiles,
    counts, visits, weight, core, factor_in, static_data, static_factor,
    core_new, feature_new, patient_new, static_new,
    vis, proj, total, codes, scales,
    gram_own, gram_parts, gram_mine, gram_all, coupled_own, coupled_parts,
    weights_all, static_all,
    mats, work, inverses, wides, row_weights, squares, grams, factors, halves, mappers, updates,
    patient_sum, patient_used, core_sum_own, core_used,
    terms_out, terms_in, core_in, new_out, new_in, coreg_out, coreg_in,
    vis_sem, line_send, line_recv,
    gram_send, gram_recv, coupled_send, coupled_recv, patient_send, patient_recv,
    core_z_send, core_z_recv, inv_send, inv_recv,
    gram_all_send, gram_all_recv, weight_send, weight_recv, static_send, static_recv,
    terms_send, terms_recv, core_send, core_recv,
    new_send, new_recv, coreg_send, coreg_recv,
):
    me = lax.axis_index("pat")
    z = lax.axis_index("feat")
    rank = core.shape[0]
    rows = visits.shape[0]
    rows_chunk = rows // chunks
    patients = weight.shape[0]
    features = visits.shape[1]
    piece = features // n_pat
    core_rows = coreg_out.shape[0]
    owners = rank // core_rows
    blocks = rows // BLK
    per_chunk = rows_chunk // BLK
    inner = z > 0
    outer = z < n_feat - 1
    lower = z < n_feat // 2
    source = n_feat // 2
    quad = 4

    def remote(src, dst, send, recv, **where):
        return pltpu.make_async_remote_copy(
            src_ref=src, dst_ref=dst, send_sem=send, recv_sem=recv,
            device_id=where, device_id_type=MESH,
        )

    def span(c):
        return pl.ds(pl.multiple_of(c * rows_chunk, rows_chunk), rows_chunk)

    def load(c):
        return pltpu.make_async_copy(visits.at[span(c)], vis.at[span(c)], vis_sem.at[c])

    def pat_peer(d):
        return lax.rem(me + d, n_pat)

    def feat_peer(d):
        return lax.rem(z + d, n_feat)

    @pl.loop(0, chunks)
    def _(c):
        load(c).start()

    barrier = pltpu.get_barrier_semaphore()
    for d in range(1, n_pat):
        pl.semaphore_signal(
            barrier, inc=1, device_id={"pat": pat_peer(d)}, device_id_type=MESH
        )
    for d in range(1, n_feat):
        pl.semaphore_signal(
            barrier, inc=1, device_id={"feat": feat_peer(d)}, device_id_type=MESH
        )

    weights_all[me] = weight[...]
    static_all[me] = static_data[...].astype(F32)
    gram_own[0] = dg(factor_in[...], factor_in[...], TN).reshape(owners, core_rows, rank)
    gram_own[1] = dg(static_factor[...], static_factor[...], TN).reshape(owners, core_rows, rank)
    coupled_own[...] = dg(static_data[...], static_factor[...], NN)
    mine = lax.rem(me, owners)
    for m in range(2):
        gram_parts[z, m] = gram_own[m, mine]
    coupled_parts[z] = coupled_own[...]

    pl.semaphore_wait(barrier, n_pat - 1 + n_feat - 1)

    def gram_copy(d):
        return remote(
            gram_parts.at[z], gram_parts.at[z], gram_send.at[d], gram_recv.at[z], feat=feat_peer(d)
        )

    def coupled_copy(d):
        return remote(
            coupled_own, coupled_parts.at[z], coupled_send.at[d], coupled_recv.at[z],
            feat=feat_peer(d),
        )

    def weight_copy(d):
        return remote(
            weights_all.at[me], weights_all.at[me], weight_send.at[d], weight_recv.at[me],
            pat=pat_peer(d),
        )

    def static_copy(d):
        return remote(
            static_all.at[me], static_all.at[me], static_send.at[d], static_recv.at[me],
            pat=pat_peer(d),
        )

    def gram_all_copy(d):
        return remote(
            gram_mine, gram_all.at[me], gram_all_send.at[d], gram_all_recv.at[me], pat=pat_peer(d)
        )

    for d in range(1, n_feat):
        gram_copy(d).start()
        coupled_copy(d).start()
    for d in range(1, n_pat):
        weight_copy(d).start()
        static_copy(d).start()

    def each_peer(fn):
        for d in range(1, n_pat):
            fn(d, pat_peer(d))

    def arrived(buffer, send, recv):
        def one(d, peer):
            remote(
                buffer.at[peer], buffer.at[peer], send.at[d], recv.at[peer], pat=peer
            ).wait_recv()

        each_peer(one)

    def arrived_z(buffer, send, recv):
        for d in range(1, n_feat):
            peer = feat_peer(d)
            remote(
                buffer.at[peer], buffer.at[peer], send.at[d], recv.at[peer], feat=peer
            ).wait_recv()

    UP_OUT, DOWN_OUT, LOW, HIGH = 0, 1, 2, 3

    def line_copies(c, up):
        way = 0 if up else 1
        out, into = (UP_OUT, LOW) if up else (DOWN_OUT, HIGH)
        peer = z + 1 if up else z - 1
        return (
            remote(
                codes.at[out, span(c)], codes.at[into, span(c)],
                line_send.at[way, 0, c], line_recv.at[way, 0, c], feat=peer,
            ),
            remote(
                scales.at[out, c], scales.at[into, c],
                line_send.at[way, 1, c], line_recv.at[way, 1, c], feat=peer,
            ),
        )

    def block_span(c, b):
        return pl.ds(pl.multiple_of(c * rows_chunk + b * BLK, BLK), BLK)

    def decode(slot, c, b):
        return codes[slot, block_span(c, b), :].astype(jnp.int32).astype(F32) * scales[
            slot, c, pl.ds(b, 1), :
        ]

    def post(c, up, values):
        slot = UP_OUT if up else DOWN_OUT
        for b in range(per_chunk):
            value = values(b)
            top = jnp.maximum(jnp.max(jnp.abs(value), axis=0, keepdims=True), 1e-30)
            code = jnp.round(value * (LEVELS / top)).astype(jnp.int32)
            codes[slot, block_span(c, b), :] = code.astype(jnp.int16)
            scales[slot, c, pl.ds(b, 1), :] = top * (1.0 / LEVELS)
        for copy in line_copies(c, up):
            copy.start()

    def relay(c, up):
        slot = LOW if up else HIGH
        for copy in line_copies(c, up):
            copy.wait_recv()

        @pl.when(outer if up else inner)
        def _():
            post(c, up, lambda b: proj[block_span(c, b), :] + decode(slot, c, b))

    def near(c):
        @pl.when(inner & lower)
        def _():
            relay(c, True)

        @pl.when(outer & jnp.logical_not(lower))
        def _():
            relay(c, False)

    def far(c):
        @pl.when(lower)
        def _():
            relay(c, False)

        @pl.when(jnp.logical_not(lower))
        def _():
            relay(c, True)

    def project(first, last):
        @pl.loop(first, last)
        def _(c):
            load(c).wait()
            proj[span(c), :] = dg(vis[span(c), :], factor_in[...], NN)

            @pl.when(z == 0)
            def _():
                post(c, True, lambda b: proj[block_span(c, b), :])

            @pl.when(z == n_feat - 1)
            def _():
                post(c, False, lambda b: proj[block_span(c, b), :])

    project(0, 4)
    arrived_z(gram_parts, gram_send, gram_recv)
    gram_mine[...] = jnp.sum(gram_parts[...], axis=0)
    gram_all[me] = gram_mine[...]
    for d in range(1, n_pat):
        gram_all_copy(d).start()
    project(4, 8)
    near(0)
    project(8, 12)
    near(1)
    project(12, chunks)

    arrived(weights_all, weight_send, weight_recv)
    arrived(gram_all, gram_all_send, gram_all_recv)

    lane = lax.broadcasted_iota(jnp.int32, (rank, rank), 1)
    sub = lax.broadcasted_iota(jnp.int32, (rank, rank), 0)
    identity = (lane == sub).astype(F32)
    all_rows = weights_all[...].reshape(n_pat * patients, rank)
    weight_gram = exact(all_rows, all_rows, TN)
    core_gram = exact(core[...], core[...], TN)
    feature_gram = jnp.concatenate([gram_all[q, 0] for q in range(owners)], axis=0)
    static_gram = jnp.concatenate([gram_all[q, 1] for q in range(owners)], axis=0)
    mats[0] = feature_gram * weight_gram + MU_RIDGE * identity
    mats[1] = core_gram * weight_gram + MU_RIDGE * identity
    mats[2] = core_gram * feature_gram + static_gram + MU_RIDGE * identity
    mats[3] = weight_gram + MU_RIDGE * identity
    which = lax.rem(me, quad)
    work[...] = mats[which]

    lane_row = lax.broadcasted_iota(jnp.int32, (1, rank), 1)
    sub_col = lax.broadcasted_iota(jnp.int32, (rank, 1), 0)

    def eliminate(k):
        whole = work[...]
        row = work[pl.ds(k, 1), :]
        pivot = jnp.sum(jnp.where(lane_row == k, row, 0.0), axis=1, keepdims=True)
        column = jnp.sum(jnp.where(lane == k, whole, 0.0), axis=1, keepdims=True)
        inverse = 1.0 / pivot
        scaled = jnp.where(lane_row == k, inverse, row * inverse)
        cleared = jnp.where((lane == k) | (sub == k), 0.0, whole)
        work[...] = cleared - jnp.where(sub_col == k, -1.0, column) * scaled

    starts, ends, lives = [], [], []
    position = jnp.int32(0)
    for k in range(patients):
        starts.append(position)
        lives.append(position + counts[k])
        position = position + ((counts[k] + (BLK - 1)) & (-BLK))
        ends.append(position)

    start_row = jnp.full((1, rank), rows, jnp.int32)
    live_row = jnp.zeros((1, rank), jnp.int32)
    patient_col = lax.broadcasted_iota(jnp.int32, (patients, 1), 0)
    start_col = jnp.full((patients, 1), rows, jnp.int32)
    end_col = jnp.zeros((patients, 1), jnp.int32)
    for k in range(patients):
        start_row = jnp.where(lane_row == k, starts[k], start_row)
        live_row = jnp.where(lane_row == k, lives[k], live_row)
        start_col = jnp.where(patient_col == k, starts[k], start_col)
        end_col = jnp.where(patient_col == k, ends[k], end_col)
    weight_pair = join(
        jnp.concatenate([weight[...], jnp.zeros((rank - patients, rank), F32)], axis=0)
    )
    chunk_row = lax.broadcasted_iota(jnp.int32, (rows_chunk, rank), 0)

    def finish(c):
        total[span(c), :] = proj[span(c), :]

        @pl.when(inner)
        def _():
            for b in range(per_chunk):
                total[block_span(c, b), :] += decode(LOW, c, b)

        @pl.when(outer)
        def _():
            for b in range(per_chunk):
                total[block_span(c, b), :] += decode(HIGH, c, b)

        at = chunk_row + c * rows_chunk
        live = jnp.where((at >= start_row) & (at < live_row), 1.0, 0.0).astype(BF16)
        by_row = halves_sum(dg(live, weight_pair, NN))
        wide = total[span(c), :] * by_row
        row_weights[span(c), :] = by_row
        wides[span(c), :] = wide
        for b in range(per_chunk):
            one = join(wide[b * BLK : (b + 1) * BLK])
            both = dg(one, one, TN)
            squares[c * per_chunk + b] = halves_sum(both[:rank] + both[rank:])

    lag = 2
    share = rank // chunks

    def eliminate_some(first):
        @pl.loop(0, share)
        def _(j):
            eliminate(first + j)

    @pl.loop(lag, chunks)
    def _(c):
        near(c)
        far(c - lag)
        finish(c - lag)
        eliminate_some((c - lag) * share)

    @pl.loop(chunks, chunks + lag)
    def _(c):
        far(c - lag)
        finish(c - lag)
        eliminate_some((c - lag) * share)

    def inv_peer(d):
        return lax.div(me, quad) * quad + lax.rem(me + d, quad)

    inverses[which] = work[...]

    def inv_copy(d):
        return remote(
            inverses.at[which], inverses.at[which], inv_send.at[d], inv_recv.at[which],
            pat=inv_peer(d),
        )

    for d in range(1, quad):
        inv_copy(d).start()

    most = MAXV // BLK
    for k in range(patients):
        first = lax.shift_right_logical(starts[k], 7)
        after = lax.shift_right_logical(ends[k], 7)
        square = squares[first]
        for i in range(1, most):
            keep = jnp.where(first + i < after, 1.0, 0.0).astype(F32)
            square = square + keep * squares[jnp.minimum(first + i, blocks - 1)]
        half = dot4(core[...], square)
        halves[k] = half
        gram = dot4_nt(half, core[...])
        trace = jnp.sum(jnp.sum(gram * identity, axis=1, keepdims=True), axis=0, keepdims=True)
        grams[k] = gram / trace
        factors[k] = identity / jnp.sqrt(trace)

    @pl.loop(0, NS_STEPS)
    def _(step):
        for k in range(patients):
            moment = grams[k]
            correction = twice(1.5 * identity - 0.5 * moment)
            both = jnp.concatenate([factors[k], moment], axis=0)
            both = halves_sum(dg(join(both), correction, NN))
            factors[k] = both[:rank]
            grams[k] = halves_sum(dg(join(both[rank:]), correction, NN))

    core_terms = jnp.zeros((rank, rank), F32)
    for k in range(patients):
        factor = factors[k]
        core_terms = core_terms + dot4_tn(factor, halves[k])
        mappers[k] = twice(dot4_tn(core[...], dot4(factor, core[...])))

    core_sum_own[...] = core_terms.reshape(owners, core_rows, rank)

    def core_z_copy(d):
        return remote(
            core_sum_own, core_used, core_z_send.at[d], core_z_recv.at[0], feat=feat_peer(d)
        )

    def patient_copy(d):
        return remote(
            patient_sum, patient_used, patient_send.at[d], patient_recv.at[0], feat=feat_peer(d)
        )

    @pl.when(z == source)
    def _():
        core_used[...] = core_sum_own[...]
        for d in range(1, n_feat):
            core_z_copy(d).start()

    group = 8
    group_rows = group * BLK

    def map_group(g, sums):
        for i in range(group):
            b = g * group + i
            at = b * BLK
            span_b = pl.ds(pl.multiple_of(at, BLK), BLK)
            owner = jnp.int32(0)
            for k in range(patients - 1):
                owner = owner + jnp.where(at >= ends[k], 1, 0)
            mapped = halves_sum(dg(join(wides[span_b, :]), mappers[owner], NN))
            products = mapped * total[span_b, :]
            updates[span_b, :] = (mapped * row_weights[span_b, :]).astype(BF16)
            member = jnp.where((at >= start_col) & (at < end_col), 1.0, 0.0).astype(F32)
            sums = sums + member * jnp.sum(products, axis=0, keepdims=True)
        return sums

    patient_sum[...] = lax.fori_loop(
        0, blocks // group, map_group, jnp.zeros((patients, rank), F32)
    )

    @pl.when(z == source)
    def _():
        patient_used[...] = patient_sum[...]
        for d in range(1, n_feat):
            patient_copy(d).start()

    for d in range(1, quad):
        peer = inv_peer(d)
        slot = lax.rem(me + d, quad)
        remote(
            inverses.at[slot], inverses.at[slot], inv_send.at[d], inv_recv.at[slot], pat=peer
        ).wait_recv()

    width = features // tiles
    per = n_pat // tiles

    def terms_copy(peer):
        return remote(
            terms_out.at[peer], terms_in.at[me], terms_send.at[peer], terms_recv.at[me], pat=peer
        )

    def core_copy(d):
        peer = pat_peer(d)
        return remote(
            core_used.at[lax.rem(peer, owners)], core_in.at[me], core_send.at[d],
            core_recv.at[me], pat=peer,
        )

    def some_tiles(first, last):
        @pl.loop(first, last)
        def _(s):
            tile = lax.rem(lax.div(me, per) + 1 + s, tiles)
            columns = pl.ds(pl.multiple_of(tile * width, width), width)
            acc = jnp.zeros((width, rank), F32)
            for g in range(blocks // group):
                acc = acc + dg(
                    vis[g * group_rows : (g + 1) * group_rows, columns],
                    updates[g * group_rows : (g + 1) * group_rows, :],
                    TN,
                )
            acc = solve(acc, mats[1], inverses[1]).astype(BF16)
            for j in range(per):
                peer = tile * per + j
                terms_out[peer] = acc[j * piece : (j + 1) * piece]

                @pl.when(peer != me)
                def _():
                    terms_copy(peer).start()

    some_tiles(0, tiles // 2)

    @pl.when(z != source)
    def _():
        core_z_copy(0).wait_recv()

    core_in[me] = core_used[mine]
    for d in range(1, n_pat):
        core_copy(d).start()

    some_tiles(tiles // 2, tiles)

    arrived(core_in, core_send, core_recv)
    terms_in[me] = terms_out[me]
    arrived(terms_in, terms_send, terms_recv)

    core_sum = jnp.sum(core_in[...], axis=0)
    coreg_out[...] = solve(core_sum, mats[0], inverses[0])
    terms_sum = jnp.sum(terms_in[...].astype(F32), axis=0)
    new_out[...] = terms_sum.astype(BF16)

    def new_copy(d):
        return remote(new_out, new_in.at[me], new_send.at[d], new_recv.at[me], pat=pat_peer(d))

    def coreg_copy(d):
        return remote(
            coreg_out, coreg_in.at[me], coreg_send.at[d], coreg_recv.at[me], pat=pat_peer(d)
        )

    for d in range(1, n_pat):
        new_copy(d).start()
        coreg_copy(d).start()
    new_in[me] = new_out[...]
    coreg_in[me] = coreg_out[...]

    @pl.when(z != source)
    def _():
        patient_copy(0).wait_recv()

    arrived_z(coupled_parts, coupled_send, coupled_recv)
    coupled = jnp.sum(coupled_parts[...], axis=0)
    patient_new[...] = solve(patient_used[...] + coupled, mats[2], inverses[2])
    arrived(static_all, static_send, static_recv)
    static_terms = exact(static_all[...].reshape(n_pat * patients, -1), all_rows, TN)
    static_new[...] = solve(static_terms, mats[3], inverses[3])

    arrived(coreg_in, coreg_send, coreg_recv)
    for q in range(owners):
        core_new[pl.ds(q * core_rows, core_rows), :] = coreg_in[q]
    arrived(new_in, new_send, new_recv)
    feature_new[...] = new_in[...].astype(F32).reshape(features, rank)

    for d in range(1, n_pat):
        weight_copy(d).wait_send()
        static_copy(d).wait_send()
        gram_all_copy(d).wait_send()
        core_copy(d).wait_send()
        new_copy(d).wait_send()
        coreg_copy(d).wait_send()
        terms_copy(pat_peer(d)).wait_send()
    for d in range(1, quad):
        inv_copy(d).wait_send()
    for d in range(1, n_feat):
        gram_copy(d).wait_send()
        coupled_copy(d).wait_send()

    @pl.when(z == source)
    def _():
        for d in range(1, n_feat):
            core_z_copy(d).wait_send()
            patient_copy(d).wait_send()

    @pl.loop(0, chunks)
    def _(c):
        @pl.when(outer)
        def _():
            for copy in line_copies(c, True):
                copy.wait_send()

        @pl.when(inner)
        def _():
            for copy in line_copies(c, False):
                copy.wait_send()


def local(n_pat, n_feat, visits, counts, weight, core, factor, static_data, static_factor):
    rows, features = visits.shape
    patients, rank = weight.shape
    columns = static_data.shape[1]
    chunks = 16
    tiles = min(n_pat, features // 128)
    core_rows = max(rank // n_pat, 16)
    owners = rank // core_rows
    piece = features // n_pat
    blocks = rows // BLK
    vmem, dma = pltpu.VMEM, pltpu.SemaphoreType.DMA
    scratch = [
        vmem((rows, features), BF16),
        vmem((rows, rank), F32),
        vmem((rows, rank), F32),
        vmem((4, rows, rank), jnp.int16),
        vmem((4, chunks, blocks // chunks, rank), F32),
        vmem((2, owners, core_rows, rank), F32),
        vmem((n_feat, 2, core_rows, rank), F32),
        vmem((2, core_rows, rank), F32),
        vmem((n_pat, 2, core_rows, rank), F32),
        vmem((patients, rank), F32),
        vmem((n_feat, patients, rank), F32),
        vmem((n_pat, patients, rank), F32),
        vmem((n_pat, patients, columns), F32),
        vmem((4, rank, rank), F32),
        vmem((rank, rank), F32),
        vmem((4, rank, rank), F32),
        vmem((rows, rank), F32),
        vmem((rows, rank), F32),
        vmem((blocks, rank, rank), F32),
        vmem((patients, rank, rank), F32),
        vmem((patients, rank, rank), F32),
        vmem((patients, rank, rank), F32),
        vmem((patients, 2 * rank, 2 * rank), BF16),
        vmem((rows, rank), BF16),
        vmem((patients, rank), F32),
        vmem((patients, rank), F32),
        vmem((owners, core_rows, rank), F32),
        vmem((owners, core_rows, rank), F32),
        vmem((n_pat, piece, rank), BF16),
        vmem((n_pat, piece, rank), BF16),
        vmem((n_pat, core_rows, rank), F32),
        vmem((piece, rank), BF16),
        vmem((n_pat, piece, rank), BF16),
        vmem((core_rows, rank), F32),
        vmem((n_pat, core_rows, rank), F32),
        dma((chunks,)),
        dma((2, 2, chunks)),
        dma((2, 2, chunks)),
    ]
    scratch += [dma((n_feat,))] * 8 + [dma((4,))] * 2 + [dma((n_pat,))] * 14
    space = pl.BlockSpec(memory_space=pltpu.VMEM)
    return pl.pallas_call(
        functools.partial(kernel, n_pat, n_feat, chunks, tiles),
        out_shape=(
            jax.ShapeDtypeStruct((rank, rank), F32),
            jax.ShapeDtypeStruct((features, rank), F32),
            jax.ShapeDtypeStruct((patients, rank), F32),
            jax.ShapeDtypeStruct((columns, rank), F32),
        ),
        in_specs=[
            pl.BlockSpec(memory_space=pltpu.SMEM),
            pl.BlockSpec(memory_space=pl.ANY),
            space, space, space, space, space,
        ],
        out_specs=(space, space, space, space),
        scratch_shapes=scratch,
        compiler_params=pltpu.CompilerParams(
            collective_id=0, has_side_effects=True, vmem_limit_bytes=62 * 1024 * 1024
        ),
        name="sweep",
    )(counts, visits, weight, core, factor, static_data, static_factor)


def solution(mesh):
    return jax.shard_map(
        functools.partial(local, mesh.shape["pat"], mesh.shape["feat"]),
        mesh=mesh,
        in_specs=(
            P("pat", "feat"),
            P("pat"),
            P("pat", None),
            P(),
            P("feat", None),
            P("pat", "feat"),
            P("feat", None),
        ),
        out_specs=(P(), P("feat", None), P("pat", None), P("feat", None)),
        check_vma=False,
    )
```

```python
import functools

import jax
import jax.numpy as jnp
from jax import lax
from jax.experimental import pallas as pl
from jax.experimental.pallas import tpu as pltpu
from jax.sharding import PartitionSpec as P

BLK = 128
NS_STEPS = 8
MU_RIDGE = 1.0
MAXV = 512
LEVELS = 32766.0
F32 = jnp.float32
BF16 = jnp.bfloat16
MESH = pl.DeviceIdType.MESH

NN = (((1,), (0,)), ((), ()))
NT = (((1,), (1,)), ((), ()))
TN = (((0,), (0,)), ((), ()))


def dg(a, b, dims):
    return lax.dot_general(a, b, dims, preferred_element_type=F32)


def split(x):
    hi = x.astype(BF16)
    return hi, (x - hi.astype(F32)).astype(BF16)


def join(x):
    return jnp.concatenate(split(x), axis=1)


def twice(x):
    wide = join(x)
    return jnp.concatenate([wide, wide], axis=0)


def halves_sum(x):
    n = x.shape[1] // 2
    return x[:, :n] + x[:, n:]


def dot4(a, b):
    return halves_sum(dg(join(a), twice(b), NN))


def dot4_nt(a, b):
    hi, lo = split(b)
    rows = jnp.concatenate(
        [jnp.concatenate([hi, hi], axis=1), jnp.concatenate([lo, lo], axis=1)], axis=0
    )
    return halves_sum(dg(join(a), rows, NT))


def dot4_tn(a, b):
    return halves_sum(dg(jnp.concatenate(split(a), axis=0), twice(b), TN))


def thirds(x):
    high = x.astype(BF16)
    rest = x - high.astype(F32)
    middle = rest.astype(BF16)
    return high, middle, (rest - middle.astype(F32)).astype(BF16)


def exact(a, b, dims=NN):
    return lax.dot_general(
        a, b, dims, precision=lax.Precision.HIGHEST, preferred_element_type=F32
    )


def solve(rhs, matrix, inverse):
    guess = dot4(rhs, inverse)
    return guess + dot4(rhs - exact(guess, matrix), inverse)


def kernel(
    n_pat, n_feat, chunks, tiles,
    counts, visits, weight, core, factor_in, static_data, static_factor,
    core_new, feature_new, patient_new, static_new,
    vis, proj, total, codes, scales,
    gram_own, gram_parts, gram_mine, gram_all, coupled_own, coupled_parts,
    weights_all, static_all,
    mats, work, inverses, wides, row_weights, squares, grams, factors, halves, mappers, updates, left,
    patient_sum, patient_used, core_sum_own, core_used,
    terms_out, terms_in, core_in, new_out, new_in, coreg_out, coreg_in,
    vis_sem, line_send, line_recv,
    gram_send, gram_recv, coupled_send, coupled_recv, patient_send, patient_recv,
    core_z_send, core_z_recv, inv_send, inv_recv,
    gram_all_send, gram_all_recv, weight_send, weight_recv, static_send, static_recv,
    terms_send, terms_recv, core_send, core_recv,
    new_send, new_recv, coreg_send, coreg_recv,
):
    me = lax.axis_index("pat")
    z = lax.axis_index("feat")
    rank = core.shape[0]
    rows = visits.shape[0]
    rows_chunk = rows // chunks
    patients = weight.shape[0]
    features = visits.shape[1]
    piece = features // n_pat
    core_rows = coreg_out.shape[0]
    owners = rank // core_rows
    blocks = rows // BLK
    per_chunk = rows_chunk // BLK
    inner = z > 0
    outer = z < n_feat - 1
    lower = z < n_feat // 2
    source = n_feat // 2
    quad = 4

    def remote(src, dst, send, recv, **where):
        return pltpu.make_async_remote_copy(
            src_ref=src, dst_ref=dst, send_sem=send, recv_sem=recv,
            device_id=where, device_id_type=MESH,
        )

    def span(c):
        return pl.ds(pl.multiple_of(c * rows_chunk, rows_chunk), rows_chunk)

    def load(c):
        return pltpu.make_async_copy(visits.at[span(c)], vis.at[span(c)], vis_sem.at[c])

    def pat_peer(d):
        return lax.rem(me + d, n_pat)

    def feat_peer(d):
        return lax.rem(z + d, n_feat)

    @pl.loop(0, chunks)
    def _(c):
        load(c).start()

    barrier = pltpu.get_barrier_semaphore()
    for d in range(1, n_pat):
        pl.semaphore_signal(
            barrier, inc=1, device_id={"pat": pat_peer(d)}, device_id_type=MESH
        )
    for d in range(1, n_feat):
        pl.semaphore_signal(
            barrier, inc=1, device_id={"feat": feat_peer(d)}, device_id_type=MESH
        )

    weights_all[me] = weight[...]
    static_all[me] = static_data[...].astype(F32)
    gram_own[0] = dg(factor_in[...], factor_in[...], TN).reshape(owners, core_rows, rank)
    gram_own[1] = dg(static_factor[...], static_factor[...], TN).reshape(owners, core_rows, rank)
    coupled_own[...] = dg(static_data[...], static_factor[...], NN)
    mine = lax.rem(me, owners)
    for m in range(2):
        gram_parts[z, m] = gram_own[m, mine]
    coupled_parts[z] = coupled_own[...]

    pl.semaphore_wait(barrier, n_pat - 1 + n_feat - 1)

    def gram_copy(d):
        return remote(
            gram_parts.at[z], gram_parts.at[z], gram_send.at[d], gram_recv.at[z], feat=feat_peer(d)
        )

    def coupled_copy(d):
        return remote(
            coupled_own, coupled_parts.at[z], coupled_send.at[d], coupled_recv.at[z],
            feat=feat_peer(d),
        )

    def weight_copy(d):
        return remote(
            weights_all.at[me], weights_all.at[me], weight_send.at[d], weight_recv.at[me],
            pat=pat_peer(d),
        )

    def static_copy(d):
        return remote(
            static_all.at[me], static_all.at[me], static_send.at[d], static_recv.at[me],
            pat=pat_peer(d),
        )

    def gram_all_copy(d):
        return remote(
            gram_mine, gram_all.at[me], gram_all_send.at[d], gram_all_recv.at[me], pat=pat_peer(d)
        )

    for d in range(1, n_feat):
        gram_copy(d).start()
        coupled_copy(d).start()
    for d in range(1, n_pat):
        weight_copy(d).start()
        static_copy(d).start()

    def each_peer(fn):
        for d in range(1, n_pat):
            fn(d, pat_peer(d))

    def arrived(buffer, send, recv):
        def one(d, peer):
            remote(
                buffer.at[peer], buffer.at[peer], send.at[d], recv.at[peer], pat=peer
            ).wait_recv()

        each_peer(one)

    def arrived_z(buffer, send, recv):
        for d in range(1, n_feat):
            peer = feat_peer(d)
            remote(
                buffer.at[peer], buffer.at[peer], send.at[d], recv.at[peer], feat=peer
            ).wait_recv()

    UP_OUT, DOWN_OUT, LOW, HIGH = 0, 1, 2, 3

    def line_copies(c, up):
        way = 0 if up else 1
        out, into = (UP_OUT, LOW) if up else (DOWN_OUT, HIGH)
        peer = z + 1 if up else z - 1
        return (
            remote(
                codes.at[out, span(c)], codes.at[into, span(c)],
                line_send.at[way, 0, c], line_recv.at[way, 0, c], feat=peer,
            ),
            remote(
                scales.at[out, c], scales.at[into, c],
                line_send.at[way, 1, c], line_recv.at[way, 1, c], feat=peer,
            ),
        )

    def block_span(c, b):
        return pl.ds(pl.multiple_of(c * rows_chunk + b * BLK, BLK), BLK)

    def decode(slot, c, b):
        return codes[slot, block_span(c, b), :].astype(jnp.int32).astype(F32) * scales[
            slot, c, pl.ds(b, 1), :
        ]

    def post(c, up, values):
        slot = UP_OUT if up else DOWN_OUT
        for b in range(per_chunk):
            value = values(b)
            top = jnp.maximum(jnp.max(jnp.abs(value), axis=0, keepdims=True), 1e-30)
            code = jnp.round(value * (LEVELS / top)).astype(jnp.int32)
            codes[slot, block_span(c, b), :] = code.astype(jnp.int16)
            scales[slot, c, pl.ds(b, 1), :] = top * (1.0 / LEVELS)
        for copy in line_copies(c, up):
            copy.start()

    def relay(c, up):
        slot = LOW if up else HIGH
        for copy in line_copies(c, up):
            copy.wait_recv()

        @pl.when(outer if up else inner)
        def _():
            post(c, up, lambda b: proj[block_span(c, b), :] + decode(slot, c, b))

    def near(c):
        @pl.when(inner & lower)
        def _():
            relay(c, True)

        @pl.when(outer & jnp.logical_not(lower))
        def _():
            relay(c, False)

    def far(c):
        @pl.when(lower)
        def _():
            relay(c, False)

        @pl.when(jnp.logical_not(lower))
        def _():
            relay(c, True)

    def project(first, last):
        @pl.loop(first, last)
        def _(c):
            load(c).wait()
            proj[span(c), :] = dg(vis[span(c), :], factor_in[...], NN)

            @pl.when(z == 0)
            def _():
                post(c, True, lambda b: proj[block_span(c, b), :])

            @pl.when(z == n_feat - 1)
            def _():
                post(c, False, lambda b: proj[block_span(c, b), :])

    project(0, 4)
    arrived_z(gram_parts, gram_send, gram_recv)
    gram_mine[...] = jnp.sum(gram_parts[...], axis=0)
    gram_all[me] = gram_mine[...]
    for d in range(1, n_pat):
        gram_all_copy(d).start()
    project(4, 8)
    near(0)
    project(8, 12)
    near(1)
    project(12, chunks)

    arrived(weights_all, weight_send, weight_recv)
    arrived(gram_all, gram_all_send, gram_all_recv)

    lane = lax.broadcasted_iota(jnp.int32, (rank, rank), 1)
    sub = lax.broadcasted_iota(jnp.int32, (rank, rank), 0)
    identity = (lane == sub).astype(F32)
    all_rows = weights_all[...].reshape(n_pat * patients, rank)
    weight_gram = exact(all_rows, all_rows, TN)
    core_gram = exact(core[...], core[...], TN)
    feature_gram = jnp.concatenate([gram_all[q, 0] for q in range(owners)], axis=0)
    static_gram = jnp.concatenate([gram_all[q, 1] for q in range(owners)], axis=0)
    mats[0] = feature_gram * weight_gram + MU_RIDGE * identity
    mats[1] = core_gram * weight_gram + MU_RIDGE * identity
    mats[2] = core_gram * feature_gram + static_gram + MU_RIDGE * identity
    mats[3] = weight_gram + MU_RIDGE * identity
    which = lax.rem(me, quad)
    work[...] = mats[which]

    lane_row = lax.broadcasted_iota(jnp.int32, (1, rank), 1)
    sub_col = lax.broadcasted_iota(jnp.int32, (rank, 1), 0)

    def eliminate(k):
        n = k + 1
        whole = work[...]
        row_a = work[pl.ds(k, 1), :]
        row_b = work[pl.ds(n, 1), :]

        def pick(row, at):
            return jnp.sum(jnp.where(lane_row == at, row, 0.0), axis=1, keepdims=True)

        aa, ab, ba, bb = pick(row_a, k), pick(row_a, n), pick(row_b, k), pick(row_b, n)
        column_a = jnp.sum(jnp.where(lane == k, whole, 0.0), axis=1, keepdims=True)
        column_b = jnp.sum(jnp.where(lane == n, whole, 0.0), axis=1, keepdims=True)
        inverse = 1.0 / (aa * bb - ab * ba)
        row_a = jnp.where(lane_row == k, 1.0, jnp.where(lane_row == n, 0.0, row_a))
        row_b = jnp.where(lane_row == n, 1.0, jnp.where(lane_row == k, 0.0, row_b))
        scaled_a = (bb * inverse) * row_a - (ab * inverse) * row_b
        scaled_b = (aa * inverse) * row_b - (ba * inverse) * row_a
        pivots = (lane == k) | (sub == k) | (lane == n) | (sub == n)
        cleared = jnp.where(pivots, 0.0, whole)
        column_a = jnp.where(sub_col == k, -1.0, jnp.where(sub_col == n, 0.0, column_a))
        column_b = jnp.where(sub_col == n, -1.0, jnp.where(sub_col == k, 0.0, column_b))
        work[...] = cleared - column_a * scaled_a - column_b * scaled_b

    starts, ends, lives = [], [], []
    position = jnp.int32(0)
    for k in range(patients):
        starts.append(position)
        lives.append(position + counts[k])
        position = position + ((counts[k] + (BLK - 1)) & (-BLK))
        ends.append(position)

    start_row = jnp.full((1, rank), rows, jnp.int32)
    live_row = jnp.zeros((1, rank), jnp.int32)
    patient_col = lax.broadcasted_iota(jnp.int32, (patients, 1), 0)
    start_col = jnp.full((patients, 1), rows, jnp.int32)
    end_col = jnp.zeros((patients, 1), jnp.int32)
    for k in range(patients):
        start_row = jnp.where(lane_row == k, starts[k], start_row)
        live_row = jnp.where(lane_row == k, lives[k], live_row)
        start_col = jnp.where(patient_col == k, starts[k], start_col)
        end_col = jnp.where(patient_col == k, ends[k], end_col)
    weight_pair = join(
        jnp.concatenate([weight[...], jnp.zeros((rank - patients, rank), F32)], axis=0)
    )
    chunk_row = lax.broadcasted_iota(jnp.int32, (rows_chunk, rank), 0)

    def finish(c):
        total[span(c), :] = proj[span(c), :]

        @pl.when(inner)
        def _():
            for b in range(per_chunk):
                total[block_span(c, b), :] += decode(LOW, c, b)

        @pl.when(outer)
        def _():
            for b in range(per_chunk):
                total[block_span(c, b), :] += decode(HIGH, c, b)

        at = chunk_row + c * rows_chunk
        live = jnp.where((at >= start_row) & (at < live_row), 1.0, 0.0).astype(BF16)
        by_row = halves_sum(dg(live, weight_pair, NN))
        wide = total[span(c), :] * by_row
        row_weights[span(c), :] = by_row
        wides[span(c), :] = wide
        for b in range(per_chunk):
            one = join(wide[b * BLK : (b + 1) * BLK])
            both = dg(one, one, TN)
            squares[c * per_chunk + b] = halves_sum(both[:rank] + both[rank:])

    lag = 2
    share = rank // chunks

    def eliminate_some(first):
        @pl.loop(0, share // 2)
        def _(j):
            eliminate(first + 2 * j)

    @pl.loop(lag, chunks)
    def _(c):
        near(c)
        far(c - lag)
        finish(c - lag)
        eliminate_some((c - lag) * share)

    @pl.loop(chunks, chunks + lag)
    def _(c):
        far(c - lag)
        finish(c - lag)
        eliminate_some((c - lag) * share)

    def inv_peer(d):
        return lax.div(me, quad) * quad + lax.rem(me + d, quad)

    inverses[which] = work[...]

    def inv_copy(d):
        return remote(
            inverses.at[which], inverses.at[which], inv_send.at[d], inv_recv.at[which],
            pat=inv_peer(d),
        )

    for d in range(1, quad):
        inv_copy(d).start()

    most = MAXV // BLK
    every = range(patients)
    sums = []
    for k in every:
        first = lax.shift_right_logical(starts[k], 7)
        after = lax.shift_right_logical(ends[k], 7)
        square = squares[first]
        for i in range(1, most):
            keep = jnp.where(first + i < after, 1.0, 0.0).astype(F32)
            square = square + keep * squares[jnp.minimum(first + i, blocks - 1)]
        sums.append(square)
    sums = [dot4(core[...], square) for square in sums]
    for k in every:
        halves[k] = sums[k]
    products = [dot4_nt(half, core[...]) for half in sums]
    for k in every:
        trace = jnp.sum(
            jnp.sum(products[k] * identity, axis=1, keepdims=True), axis=0, keepdims=True
        )
        grams[k] = products[k] / trace
        factors[k] = identity / jnp.sqrt(trace)

    def corrections():
        return [twice(1.5 * identity - 0.5 * grams[k]) for k in every]

    @pl.loop(0, NS_STEPS - 1)
    def _(step):
        rights, firsts = [], []
        for k in every:
            moment = grams[k]
            right = twice(1.5 * identity - 0.5 * moment)
            both = jnp.concatenate([factors[k], moment], axis=0)
            rights.append(right)
            firsts.append(dg(join(both), right, NN))
        for k in every:
            both = halves_sum(firsts[k])
            factors[k] = both[:rank]
            grams[k] = halves_sum(dg(join(both[rank:]), rights[k], NN))

    rights = corrections()
    lasts = [halves_sum(dg(join(factors[k]), rights[k], NN)) for k in every]
    mapped_core = [dot4(factor, core[...]) for factor in lasts]
    for k in every:
        mappers[k] = twice(dot4_tn(core[...], mapped_core[k]))
    parts = [dot4_tn(lasts[k], halves[k]) for k in every]
    core_terms = parts[0]
    for k in range(1, patients):
        core_terms = core_terms + parts[k]

    core_sum_own[...] = core_terms.reshape(owners, core_rows, rank)

    def core_z_copy(d):
        return remote(
            core_sum_own, core_used, core_z_send.at[d], core_z_recv.at[0], feat=feat_peer(d)
        )

    def patient_copy(d):
        return remote(
            patient_sum, patient_used, patient_send.at[d], patient_recv.at[0], feat=feat_peer(d)
        )

    @pl.when(z == source)
    def _():
        core_used[...] = core_sum_own[...]
        for d in range(1, n_feat):
            core_z_copy(d).start()

    group = 8

    def map_group(g, sums):
        raw = []
        for i in range(group):
            at = (g * group + i) * BLK
            owner = jnp.int32(0)
            for k in range(patients - 1):
                owner = owner + jnp.where(at >= ends[k], 1, 0)
            wide = wides[pl.ds(pl.multiple_of(at, BLK), BLK), :]
            raw.append(dg(join(wide), mappers[owner], NN))
        for i in range(group):
            at = (g * group + i) * BLK
            span_b = pl.ds(pl.multiple_of(at, BLK), BLK)
            mapped = halves_sum(raw[i])
            products = mapped * total[span_b, :]
            updates[:, span_b] = jnp.transpose(mapped * row_weights[span_b, :]).astype(BF16)
            member = jnp.where((at >= start_col) & (at < end_col), 1.0, 0.0).astype(F32)
            sums = sums + member * jnp.sum(products, axis=0, keepdims=True)
        return sums

    patient_sum[...] = lax.fori_loop(
        0, blocks // group, map_group, jnp.zeros((patients, rank), F32)
    )

    @pl.when(z == source)
    def _():
        patient_used[...] = patient_sum[...]
        for d in range(1, n_feat):
            patient_copy(d).start()

    for d in range(1, quad):
        peer = inv_peer(d)
        slot = lax.rem(me + d, quad)
        remote(
            inverses.at[slot], inverses.at[slot], inv_send.at[d], inv_recv.at[slot], pat=peer
        ).wait_recv()

    width = features // tiles
    per = n_pat // tiles

    def terms_copy(peer):
        return remote(
            terms_out.at[peer], terms_in.at[me], terms_send.at[peer], terms_recv.at[me], pat=peer
        )

    def core_copy(d):
        peer = pat_peer(d)
        return remote(
            core_used.at[lax.rem(peer, owners)], core_in.at[me], core_send.at[d],
            core_recv.at[me], pat=peer,
        )

    def some_tiles(first, last):
        @pl.loop(first, last)
        def _(s):
            tile = lax.rem(lax.div(me, per) + 1 + s, tiles)
            columns = pl.ds(pl.multiple_of(tile * width, width), width)
            high, middle, low = thirds(dg(updates[...], vis[:, columns], NN))
            right = jnp.concatenate([high, high, middle, middle, low, high], axis=0)
            acc = jnp.transpose(dg(left[...], right, NN)).astype(BF16)
            for j in range(per):
                peer = tile * per + j
                terms_out[peer] = acc[j * piece : (j + 1) * piece]

                @pl.when(peer != me)
                def _():
                    terms_copy(peer).start()

    high, middle, low = thirds(inverses[1])
    left[...] = jnp.concatenate([high, middle, high, middle, high, low], axis=1)

    some_tiles(0, tiles // 2)

    @pl.when(z != source)
    def _():
        core_z_copy(0).wait_recv()

    core_in[me] = core_used[mine]
    for d in range(1, n_pat):
        core_copy(d).start()

    some_tiles(tiles // 2, tiles)

    arrived(core_in, core_send, core_recv)
    terms_in[me] = terms_out[me]
    arrived(terms_in, terms_send, terms_recv)

    core_sum = jnp.sum(core_in[...], axis=0)
    coreg_out[...] = solve(core_sum, mats[0], inverses[0])
    terms_sum = jnp.sum(terms_in[...].astype(F32), axis=0)
    new_out[...] = terms_sum.astype(BF16)

    def new_copy(d):
        return remote(new_out, new_in.at[me], new_send.at[d], new_recv.at[me], pat=pat_peer(d))

    def coreg_copy(d):
        return remote(
            coreg_out, coreg_in.at[me], coreg_send.at[d], coreg_recv.at[me], pat=pat_peer(d)
        )

    for d in range(1, n_pat):
        new_copy(d).start()
        coreg_copy(d).start()
    new_in[me] = new_out[...]
    coreg_in[me] = coreg_out[...]

    @pl.when(z != source)
    def _():
        patient_copy(0).wait_recv()

    arrived_z(coupled_parts, coupled_send, coupled_recv)
    coupled = jnp.sum(coupled_parts[...], axis=0)
    patient_new[...] = solve(patient_used[...] + coupled, mats[2], inverses[2])
    arrived(static_all, static_send, static_recv)
    static_terms = exact(static_all[...].reshape(n_pat * patients, -1), all_rows, TN)
    static_new[...] = solve(static_terms, mats[3], inverses[3])

    arrived(coreg_in, coreg_send, coreg_recv)
    for q in range(owners):
        core_new[pl.ds(q * core_rows, core_rows), :] = coreg_in[q]
    arrived(new_in, new_send, new_recv)
    feature_new[...] = new_in[...].astype(F32).reshape(features, rank)

    for d in range(1, n_pat):
        weight_copy(d).wait_send()
        static_copy(d).wait_send()
        gram_all_copy(d).wait_send()
        core_copy(d).wait_send()
        new_copy(d).wait_send()
        coreg_copy(d).wait_send()
        terms_copy(pat_peer(d)).wait_send()
    for d in range(1, quad):
        inv_copy(d).wait_send()
    for d in range(1, n_feat):
        gram_copy(d).wait_send()
        coupled_copy(d).wait_send()

    @pl.when(z == source)
    def _():
        for d in range(1, n_feat):
            core_z_copy(d).wait_send()
            patient_copy(d).wait_send()

    @pl.loop(0, chunks)
    def _(c):
        @pl.when(outer)
        def _():
            for copy in line_copies(c, True):
                copy.wait_send()

        @pl.when(inner)
        def _():
            for copy in line_copies(c, False):
                copy.wait_send()


def local(n_pat, n_feat, visits, counts, weight, core, factor, static_data, static_factor):
    rows, features = visits.shape
    patients, rank = weight.shape
    columns = static_data.shape[1]
    chunks = 16
    tiles = max(features // 512, 1)
    core_rows = max(rank // n_pat, 16)
    owners = rank // core_rows
    piece = features // n_pat
    blocks = rows // BLK
    vmem, dma = pltpu.VMEM, pltpu.SemaphoreType.DMA
    scratch = [
        vmem((rows, features), BF16),
        vmem((rows, rank), F32),
        vmem((rows, rank), F32),
        vmem((4, rows, rank), jnp.int16),
        vmem((4, chunks, blocks // chunks, rank), F32),
        vmem((2, owners, core_rows, rank), F32),
        vmem((n_feat, 2, core_rows, rank), F32),
        vmem((2, core_rows, rank), F32),
        vmem((n_pat, 2, core_rows, rank), F32),
        vmem((patients, rank), F32),
        vmem((n_feat, patients, rank), F32),
        vmem((n_pat, patients, rank), F32),
        vmem((n_pat, patients, columns), F32),
        vmem((4, rank, rank), F32),
        vmem((rank, rank), F32),
        vmem((4, rank, rank), F32),
        vmem((rows, rank), F32),
        vmem((rows, rank), F32),
        vmem((blocks, rank, rank), F32),
        vmem((patients, rank, rank), F32),
        vmem((patients, rank, rank), F32),
        vmem((patients, rank, rank), F32),
        vmem((patients, 2 * rank, 2 * rank), BF16),
        vmem((rank, rows), BF16),
        vmem((rank, 6 * rank), BF16),
        vmem((patients, rank), F32),
        vmem((patients, rank), F32),
        vmem((owners, core_rows, rank), F32),
        vmem((owners, core_rows, rank), F32),
        vmem((n_pat, piece, rank), BF16),
        vmem((n_pat, piece, rank), BF16),
        vmem((n_pat, core_rows, rank), F32),
        vmem((piece, rank), BF16),
        vmem((n_pat, piece, rank), BF16),
        vmem((core_rows, rank), F32),
        vmem((n_pat, core_rows, rank), F32),
        dma((chunks,)),
        dma((2, 2, chunks)),
        dma((2, 2, chunks)),
    ]
    scratch += [dma((n_feat,))] * 8 + [dma((4,))] * 2 + [dma((n_pat,))] * 14
    space = pl.BlockSpec(memory_space=pltpu.VMEM)
    return pl.pallas_call(
        functools.partial(kernel, n_pat, n_feat, chunks, tiles),
        out_shape=(
            jax.ShapeDtypeStruct((rank, rank), F32),
            jax.ShapeDtypeStruct((features, rank), F32),
            jax.ShapeDtypeStruct((patients, rank), F32),
            jax.ShapeDtypeStruct((columns, rank), F32),
        ),
        in_specs=[
            pl.BlockSpec(memory_space=pltpu.SMEM),
            pl.BlockSpec(memory_space=pl.ANY),
            space, space, space, space, space,
        ],
        out_specs=(space, space, space, space),
        scratch_shapes=scratch,
        compiler_params=pltpu.CompilerParams(
            collective_id=0, has_side_effects=True, vmem_limit_bytes=62 * 1024 * 1024
        ),
        name="sweep",
    )(counts, visits, weight, core, factor, static_data, static_factor)


def solution(mesh):
    return jax.shard_map(
        functools.partial(local, mesh.shape["pat"], mesh.shape["feat"]),
        mesh=mesh,
        in_specs=(
            P("pat", "feat"),
            P("pat"),
            P("pat", None),
            P(),
            P("feat", None),
            P("pat", "feat"),
            P("feat", None),
        ),
        out_specs=(P(), P("feat", None), P("pat", None), P("feat", None)),
        check_vma=False,
    )
```

```python
import functools

import jax
import jax.numpy as jnp
from jax import lax
from jax.experimental import pallas as pl
from jax.experimental.pallas import tpu as pltpu
from jax.sharding import PartitionSpec as P

BLK = 128
NS_STEPS = 8
MU_RIDGE = 1.0
MAXV = 512
LEVELS = 32766.0
F32 = jnp.float32
BF16 = jnp.bfloat16
MESH = pl.DeviceIdType.MESH

NN = (((1,), (0,)), ((), ()))
NT = (((1,), (1,)), ((), ()))
TN = (((0,), (0,)), ((), ()))


def dg(a, b, dims):
    return lax.dot_general(a, b, dims, preferred_element_type=F32)


def split(x):
    hi = x.astype(BF16)
    return hi, (x - hi.astype(F32)).astype(BF16)


def join(x):
    return jnp.concatenate(split(x), axis=1)


def twice(x):
    wide = join(x)
    return jnp.concatenate([wide, wide], axis=0)


def halves_sum(x):
    n = x.shape[1] // 2
    return x[:, :n] + x[:, n:]


def dot4(a, b):
    return halves_sum(dg(join(a), twice(b), NN))


def dot4_nt(a, b):
    hi, lo = split(b)
    rows = jnp.concatenate(
        [jnp.concatenate([hi, hi], axis=1), jnp.concatenate([lo, lo], axis=1)], axis=0
    )
    return halves_sum(dg(join(a), rows, NT))


def dot4_tn(a, b):
    return halves_sum(dg(jnp.concatenate(split(a), axis=0), twice(b), TN))


def thirds(x):
    high = x.astype(BF16)
    rest = x - high.astype(F32)
    middle = rest.astype(BF16)
    return high, middle, (rest - middle.astype(F32)).astype(BF16)


def exact(a, b, dims=NN):
    return lax.dot_general(
        a, b, dims, precision=lax.Precision.HIGHEST, preferred_element_type=F32
    )


def solve(rhs, matrix, inverse):
    guess = dot4(rhs, inverse)
    return guess + dot4(rhs - exact(guess, matrix), inverse)


def kernel(
    n_pat, n_feat, chunks, tiles,
    counts, visits, weight_hbm, core_hbm, factor_hbm, data_hbm, static_hbm,
    core_new, feature_new, patient_new, static_new,
    weight, core, factor_in, static_data, static_factor, input_sem,
    vis, proj, total, codes, scales,
    gram_own, gram_parts, gram_mine, gram_all, coupled_own, coupled_parts,
    weights_all, static_all,
    mats, work, inverses, wides, row_weights, squares, grams, factors, halves, mappers, updates, left,
    patient_sum, patient_used, core_sum_own, core_used,
    terms_out, terms_in, core_in, new_out, new_in, coreg_out, coreg_in,
    vis_sem, line_send, line_recv,
    gram_send, gram_recv, coupled_send, coupled_recv, patient_send, patient_recv,
    core_z_send, core_z_recv, inv_send, inv_recv,
    gram_all_send, gram_all_recv, weight_send, weight_recv, static_send, static_recv,
    terms_send, terms_recv, core_send, core_recv,
    new_send, new_recv, coreg_send, coreg_recv,
):
    me = lax.axis_index("pat")
    z = lax.axis_index("feat")
    rank = core.shape[0]
    rows = visits.shape[0]
    rows_chunk = rows // chunks
    patients = weight.shape[0]
    features = visits.shape[1]
    piece = features // n_pat
    core_rows = coreg_out.shape[0]
    owners = rank // core_rows
    blocks = rows // BLK
    per_chunk = rows_chunk // BLK
    inner = z > 0
    outer = z < n_feat - 1
    lower = z < n_feat // 2
    source = n_feat // 2
    quad = 4

    def remote(src, dst, send, recv, **where):
        return pltpu.make_async_remote_copy(
            src_ref=src, dst_ref=dst, send_sem=send, recv_sem=recv,
            device_id=where, device_id_type=MESH,
        )

    def span(c):
        return pl.ds(pl.multiple_of(c * rows_chunk, rows_chunk), rows_chunk)

    def load(c):
        return pltpu.make_async_copy(visits.at[span(c)], vis.at[span(c)], vis_sem.at[c])

    def pat_peer(d):
        return lax.rem(me + d, n_pat)

    def feat_peer(d):
        return lax.rem(z + d, n_feat)

    inputs = [
        pltpu.make_async_copy(source_ref, held, input_sem.at[i])
        for i, (source_ref, held) in enumerate(
            (
                (factor_hbm, factor_in), (static_hbm, static_factor), (data_hbm, static_data),
                (weight_hbm, weight), (core_hbm, core),
            )
        )
    ]
    for copy in inputs:
        copy.start()

    @pl.loop(0, chunks)
    def _(c):
        load(c).start()

    barrier = pltpu.get_barrier_semaphore()
    for d in range(1, n_pat):
        pl.semaphore_signal(
            barrier, inc=1, device_id={"pat": pat_peer(d)}, device_id_type=MESH
        )
    for d in range(1, n_feat):
        pl.semaphore_signal(
            barrier, inc=1, device_id={"feat": feat_peer(d)}, device_id_type=MESH
        )

    for copy in inputs:
        copy.wait()
    weights_all[me] = weight[...]
    static_all[me] = static_data[...].astype(F32)
    gram_own[0] = dg(factor_in[...], factor_in[...], TN).reshape(owners, core_rows, rank)
    gram_own[1] = dg(static_factor[...], static_factor[...], TN).reshape(owners, core_rows, rank)
    coupled_own[...] = dg(static_data[...], static_factor[...], NN)
    mine = lax.rem(me, owners)
    for m in range(2):
        gram_parts[z, m] = gram_own[m, mine]
    coupled_parts[z] = coupled_own[...]

    pl.semaphore_wait(barrier, n_pat - 1 + n_feat - 1)

    def gram_copy(d):
        return remote(
            gram_parts.at[z], gram_parts.at[z], gram_send.at[d], gram_recv.at[z], feat=feat_peer(d)
        )

    def coupled_copy(d):
        return remote(
            coupled_own, coupled_parts.at[z], coupled_send.at[d], coupled_recv.at[z],
            feat=feat_peer(d),
        )

    def weight_copy(d):
        return remote(
            weights_all.at[me], weights_all.at[me], weight_send.at[d], weight_recv.at[me],
            pat=pat_peer(d),
        )

    def static_copy(d):
        return remote(
            static_all.at[me], static_all.at[me], static_send.at[d], static_recv.at[me],
            pat=pat_peer(d),
        )

    def gram_all_copy(d):
        return remote(
            gram_mine, gram_all.at[me], gram_all_send.at[d], gram_all_recv.at[me], pat=pat_peer(d)
        )

    for d in range(1, n_feat):
        gram_copy(d).start()
        coupled_copy(d).start()
    for d in range(1, n_pat):
        weight_copy(d).start()
        static_copy(d).start()

    def each_peer(fn):
        for d in range(1, n_pat):
            fn(d, pat_peer(d))

    def arrived(buffer, send, recv):
        def one(d, peer):
            remote(
                buffer.at[peer], buffer.at[peer], send.at[d], recv.at[peer], pat=peer
            ).wait_recv()

        each_peer(one)

    def arrived_z(buffer, send, recv):
        for d in range(1, n_feat):
            peer = feat_peer(d)
            remote(
                buffer.at[peer], buffer.at[peer], send.at[d], recv.at[peer], feat=peer
            ).wait_recv()

    UP_OUT, DOWN_OUT, LOW, HIGH = 0, 1, 2, 3

    def line_copies(c, up):
        way = 0 if up else 1
        out, into = (UP_OUT, LOW) if up else (DOWN_OUT, HIGH)
        peer = z + 1 if up else z - 1
        return (
            remote(
                codes.at[out, span(c)], codes.at[into, span(c)],
                line_send.at[way, 0, c], line_recv.at[way, 0, c], feat=peer,
            ),
            remote(
                scales.at[out, c], scales.at[into, c],
                line_send.at[way, 1, c], line_recv.at[way, 1, c], feat=peer,
            ),
        )

    def block_span(c, b):
        return pl.ds(pl.multiple_of(c * rows_chunk + b * BLK, BLK), BLK)

    def decode(slot, c, b):
        return codes[slot, block_span(c, b), :].astype(jnp.int32).astype(F32) * scales[
            slot, c, pl.ds(b, 1), :
        ]

    def post(c, up, values):
        slot = UP_OUT if up else DOWN_OUT
        for b in range(per_chunk):
            value = values(b)
            top = jnp.maximum(jnp.max(jnp.abs(value), axis=0, keepdims=True), 1e-30)
            code = jnp.round(value * (LEVELS / top)).astype(jnp.int32)
            codes[slot, block_span(c, b), :] = code.astype(jnp.int16)
            scales[slot, c, pl.ds(b, 1), :] = top * (1.0 / LEVELS)
        for copy in line_copies(c, up):
            copy.start()

    def relay(c, up):
        slot = LOW if up else HIGH
        for copy in line_copies(c, up):
            copy.wait_recv()

        @pl.when(outer if up else inner)
        def _():
            post(c, up, lambda b: proj[block_span(c, b), :] + decode(slot, c, b))

    def near(c):
        @pl.when(inner & lower)
        def _():
            relay(c, True)

        @pl.when(outer & jnp.logical_not(lower))
        def _():
            relay(c, False)

    def far(c):
        @pl.when(lower)
        def _():
            relay(c, False)

        @pl.when(jnp.logical_not(lower))
        def _():
            relay(c, True)

    def project(first, last):
        @pl.loop(first // 2, last // 2)
        def _(p):
            load(2 * p).wait()
            load(2 * p + 1).wait()
            both = pl.ds(pl.multiple_of(p * 2 * rows_chunk, rows_chunk), 2 * rows_chunk)
            proj[both, :] = dg(vis[both, :], factor_in[...], NN)

            @pl.when(z == 0)
            def _():
                for i in range(2):
                    post(2 * p + i, True, lambda b, i=i: proj[block_span(2 * p + i, b), :])

            @pl.when(z == n_feat - 1)
            def _():
                for i in range(2):
                    post(2 * p + i, False, lambda b, i=i: proj[block_span(2 * p + i, b), :])

    project(0, 6)
    arrived_z(gram_parts, gram_send, gram_recv)
    gram_mine[...] = jnp.sum(gram_parts[...], axis=0)
    gram_all[me] = gram_mine[...]
    for d in range(1, n_pat):
        gram_all_copy(d).start()
    project(6, 10)
    near(0)
    project(10, 14)
    near(1)
    project(14, chunks)

    arrived(weights_all, weight_send, weight_recv)
    arrived(gram_all, gram_all_send, gram_all_recv)

    lane = lax.broadcasted_iota(jnp.int32, (rank, rank), 1)
    sub = lax.broadcasted_iota(jnp.int32, (rank, rank), 0)
    identity = (lane == sub).astype(F32)
    all_rows = weights_all[...].reshape(n_pat * patients, rank)
    weight_gram = exact(all_rows, all_rows, TN)
    core_gram = exact(core[...], core[...], TN)
    feature_gram = jnp.concatenate([gram_all[q, 0] for q in range(owners)], axis=0)
    static_gram = jnp.concatenate([gram_all[q, 1] for q in range(owners)], axis=0)
    mats[0] = feature_gram * weight_gram + MU_RIDGE * identity
    mats[1] = core_gram * weight_gram + MU_RIDGE * identity
    mats[2] = core_gram * feature_gram + static_gram + MU_RIDGE * identity
    mats[3] = weight_gram + MU_RIDGE * identity
    which = lax.rem(me, quad)
    work[...] = mats[which]

    lane_row = lax.broadcasted_iota(jnp.int32, (1, rank), 1)
    sub_col = lax.broadcasted_iota(jnp.int32, (rank, 1), 0)

    def eliminate(k):
        n = k + 1
        whole = work[...]
        row_a = work[pl.ds(k, 1), :]
        row_b = work[pl.ds(n, 1), :]

        def pick(row, at):
            return jnp.sum(jnp.where(lane_row == at, row, 0.0), axis=1, keepdims=True)

        aa, ab, ba, bb = pick(row_a, k), pick(row_a, n), pick(row_b, k), pick(row_b, n)
        column_a = jnp.sum(jnp.where(lane == k, whole, 0.0), axis=1, keepdims=True)
        column_b = jnp.sum(jnp.where(lane == n, whole, 0.0), axis=1, keepdims=True)
        inverse = 1.0 / (aa * bb - ab * ba)
        row_a = jnp.where(lane_row == k, 1.0, jnp.where(lane_row == n, 0.0, row_a))
        row_b = jnp.where(lane_row == n, 1.0, jnp.where(lane_row == k, 0.0, row_b))
        scaled_a = (bb * inverse) * row_a - (ab * inverse) * row_b
        scaled_b = (aa * inverse) * row_b - (ba * inverse) * row_a
        pivots = (lane == k) | (sub == k) | (lane == n) | (sub == n)
        cleared = jnp.where(pivots, 0.0, whole)
        column_a = jnp.where(sub_col == k, -1.0, jnp.where(sub_col == n, 0.0, column_a))
        column_b = jnp.where(sub_col == n, -1.0, jnp.where(sub_col == k, 0.0, column_b))
        work[...] = cleared - column_a * scaled_a - column_b * scaled_b

    starts, ends, lives = [], [], []
    position = jnp.int32(0)
    for k in range(patients):
        starts.append(position)
        lives.append(position + counts[k])
        position = position + ((counts[k] + (BLK - 1)) & (-BLK))
        ends.append(position)

    start_row = jnp.full((1, rank), rows, jnp.int32)
    live_row = jnp.zeros((1, rank), jnp.int32)
    patient_col = lax.broadcasted_iota(jnp.int32, (patients, 1), 0)
    start_col = jnp.full((patients, 1), rows, jnp.int32)
    end_col = jnp.zeros((patients, 1), jnp.int32)
    for k in range(patients):
        start_row = jnp.where(lane_row == k, starts[k], start_row)
        live_row = jnp.where(lane_row == k, lives[k], live_row)
        start_col = jnp.where(patient_col == k, starts[k], start_col)
        end_col = jnp.where(patient_col == k, ends[k], end_col)
    weight_pair = join(
        jnp.concatenate([weight[...], jnp.zeros((rank - patients, rank), F32)], axis=0)
    )
    chunk_row = lax.broadcasted_iota(jnp.int32, (rows_chunk, rank), 0)

    def finish(c):
        total[span(c), :] = proj[span(c), :]

        @pl.when(inner)
        def _():
            for b in range(per_chunk):
                total[block_span(c, b), :] += decode(LOW, c, b)

        @pl.when(outer)
        def _():
            for b in range(per_chunk):
                total[block_span(c, b), :] += decode(HIGH, c, b)

        at = chunk_row + c * rows_chunk
        live = jnp.where((at >= start_row) & (at < live_row), 1.0, 0.0).astype(BF16)
        by_row = halves_sum(dg(live, weight_pair, NN))
        wide = total[span(c), :] * by_row
        row_weights[span(c), :] = by_row
        wides[span(c), :] = wide
        for b in range(per_chunk):
            one = join(wide[b * BLK : (b + 1) * BLK])
            both = dg(one, one, TN)
            squares[c * per_chunk + b] = halves_sum(both[:rank] + both[rank:])

    lag = 2
    share = rank // chunks

    def eliminate_some(first):
        @pl.loop(0, share // 2)
        def _(j):
            eliminate(first + 2 * j)

    @pl.loop(lag, chunks)
    def _(c):
        near(c)
        far(c - lag)
        finish(c - lag)
        eliminate_some((c - lag) * share)

    @pl.loop(chunks, chunks + lag)
    def _(c):
        far(c - lag)
        finish(c - lag)
        eliminate_some((c - lag) * share)

    def inv_peer(d):
        return lax.div(me, quad) * quad + lax.rem(me + d, quad)

    inverses[which] = work[...]

    def inv_copy(d):
        return remote(
            inverses.at[which], inverses.at[which], inv_send.at[d], inv_recv.at[which],
            pat=inv_peer(d),
        )

    for d in range(1, quad):
        inv_copy(d).start()

    most = MAXV // BLK
    every = range(patients)
    sums = []
    for k in every:
        first = lax.shift_right_logical(starts[k], 7)
        after = lax.shift_right_logical(ends[k], 7)
        square = squares[first]
        for i in range(1, most):
            keep = jnp.where(first + i < after, 1.0, 0.0).astype(F32)
            square = square + keep * squares[jnp.minimum(first + i, blocks - 1)]
        sums.append(square)
    sums = [dot4(core[...], square) for square in sums]
    for k in every:
        halves[k] = sums[k]
    products = [dot4_nt(half, core[...]) for half in sums]
    for k in every:
        trace = jnp.sum(
            jnp.sum(products[k] * identity, axis=1, keepdims=True), axis=0, keepdims=True
        )
        grams[k] = products[k] / trace
        factors[k] = identity / jnp.sqrt(trace)

    def corrections():
        return [twice(1.5 * identity - 0.5 * grams[k]) for k in every]

    @pl.loop(0, NS_STEPS - 1)
    def _(step):
        rights, firsts = [], []
        for k in every:
            moment = grams[k]
            right = twice(1.5 * identity - 0.5 * moment)
            both = jnp.concatenate([factors[k], moment], axis=0)
            rights.append(right)
            firsts.append(dg(join(both), right, NN))
        for k in every:
            both = halves_sum(firsts[k])
            factors[k] = both[:rank]
            grams[k] = halves_sum(dg(join(both[rank:]), rights[k], NN))

    rights = corrections()
    lasts = [halves_sum(dg(join(factors[k]), rights[k], NN)) for k in every]
    mapped_core = [dot4(factor, core[...]) for factor in lasts]
    for k in every:
        mappers[k] = twice(dot4_tn(core[...], mapped_core[k]))
    parts = [dot4_tn(lasts[k], halves[k]) for k in every]
    core_terms = parts[0]
    for k in range(1, patients):
        core_terms = core_terms + parts[k]

    core_sum_own[...] = core_terms.reshape(owners, core_rows, rank)

    def core_z_copy(d):
        return remote(
            core_sum_own, core_used, core_z_send.at[d], core_z_recv.at[0], feat=feat_peer(d)
        )

    def patient_copy(d):
        return remote(
            patient_sum, patient_used, patient_send.at[d], patient_recv.at[0], feat=feat_peer(d)
        )

    @pl.when(z == source)
    def _():
        core_used[...] = core_sum_own[...]
        for d in range(1, n_feat):
            core_z_copy(d).start()

    group = 8

    def map_group(g, sums):
        raw = []
        for i in range(group):
            at = (g * group + i) * BLK
            owner = jnp.int32(0)
            for k in range(patients - 1):
                owner = owner + jnp.where(at >= ends[k], 1, 0)
            wide = wides[pl.ds(pl.multiple_of(at, BLK), BLK), :]
            raw.append(dg(join(wide), mappers[owner], NN))
        for i in range(group):
            at = (g * group + i) * BLK
            span_b = pl.ds(pl.multiple_of(at, BLK), BLK)
            mapped = halves_sum(raw[i])
            products = mapped * total[span_b, :]
            updates[:, span_b] = jnp.transpose(mapped * row_weights[span_b, :]).astype(BF16)
            member = jnp.where((at >= start_col) & (at < end_col), 1.0, 0.0).astype(F32)
            sums = sums + member * jnp.sum(products, axis=0, keepdims=True)
        return sums

    patient_sum[...] = lax.fori_loop(
        0, blocks // group, map_group, jnp.zeros((patients, rank), F32)
    )

    @pl.when(z == source)
    def _():
        patient_used[...] = patient_sum[...]
        for d in range(1, n_feat):
            patient_copy(d).start()

    for d in range(1, quad):
        peer = inv_peer(d)
        slot = lax.rem(me + d, quad)
        remote(
            inverses.at[slot], inverses.at[slot], inv_send.at[d], inv_recv.at[slot], pat=peer
        ).wait_recv()

    width = features // tiles
    per = n_pat // tiles

    def terms_copy(peer):
        return remote(
            terms_out.at[peer], terms_in.at[me], terms_send.at[peer], terms_recv.at[me], pat=peer
        )

    def core_copy(d):
        peer = pat_peer(d)
        return remote(
            core_used.at[lax.rem(peer, owners)], core_in.at[me], core_send.at[d],
            core_recv.at[me], pat=peer,
        )

    def some_tiles(first, last):
        @pl.loop(first, last)
        def _(s):
            tile = lax.rem(lax.div(me, per) + 1 + s, tiles)
            columns = pl.ds(pl.multiple_of(tile * width, width), width)
            high, middle, low = thirds(dg(updates[...], vis[:, columns], NN))
            right = jnp.concatenate([high, high, middle, middle, low, high], axis=0)
            acc = jnp.transpose(dg(left[...], right, NN)).astype(BF16)
            for j in range(per):
                peer = tile * per + j
                terms_out[peer] = acc[j * piece : (j + 1) * piece]

                @pl.when(peer != me)
                def _():
                    terms_copy(peer).start()

    high, middle, low = thirds(inverses[1])
    left[...] = jnp.concatenate([high, middle, high, middle, high, low], axis=1)

    some_tiles(0, tiles // 2)

    @pl.when(z != source)
    def _():
        core_z_copy(0).wait_recv()

    core_in[me] = core_used[mine]
    for d in range(1, n_pat):
        core_copy(d).start()

    some_tiles(tiles // 2, tiles)

    arrived(core_in, core_send, core_recv)
    terms_in[me] = terms_out[me]
    arrived(terms_in, terms_send, terms_recv)

    core_sum = jnp.sum(core_in[...], axis=0)
    coreg_out[...] = solve(core_sum, mats[0], inverses[0])
    terms_sum = jnp.sum(terms_in[...].astype(F32), axis=0)
    new_out[...] = terms_sum.astype(BF16)

    def new_copy(d):
        return remote(new_out, new_in.at[me], new_send.at[d], new_recv.at[me], pat=pat_peer(d))

    def coreg_copy(d):
        return remote(
            coreg_out, coreg_in.at[me], coreg_send.at[d], coreg_recv.at[me], pat=pat_peer(d)
        )

    for d in range(1, n_pat):
        new_copy(d).start()
        coreg_copy(d).start()
    new_in[me] = new_out[...]
    coreg_in[me] = coreg_out[...]

    @pl.when(z != source)
    def _():
        patient_copy(0).wait_recv()

    arrived_z(coupled_parts, coupled_send, coupled_recv)
    coupled = jnp.sum(coupled_parts[...], axis=0)
    patient_new[...] = solve(patient_used[...] + coupled, mats[2], inverses[2])
    arrived(static_all, static_send, static_recv)
    static_terms = exact(static_all[...].reshape(n_pat * patients, -1), all_rows, TN)
    static_new[...] = solve(static_terms, mats[3], inverses[3])

    arrived(coreg_in, coreg_send, coreg_recv)
    for q in range(owners):
        core_new[pl.ds(q * core_rows, core_rows), :] = coreg_in[q]
    arrived(new_in, new_send, new_recv)
    feature_new[...] = new_in[...].astype(F32).reshape(features, rank)

    for d in range(1, n_pat):
        weight_copy(d).wait_send()
        static_copy(d).wait_send()
        gram_all_copy(d).wait_send()
        core_copy(d).wait_send()
        new_copy(d).wait_send()
        coreg_copy(d).wait_send()
        terms_copy(pat_peer(d)).wait_send()
    for d in range(1, quad):
        inv_copy(d).wait_send()
    for d in range(1, n_feat):
        gram_copy(d).wait_send()
        coupled_copy(d).wait_send()

    @pl.when(z == source)
    def _():
        for d in range(1, n_feat):
            core_z_copy(d).wait_send()
            patient_copy(d).wait_send()

    @pl.loop(0, chunks)
    def _(c):
        @pl.when(outer)
        def _():
            for copy in line_copies(c, True):
                copy.wait_send()

        @pl.when(inner)
        def _():
            for copy in line_copies(c, False):
                copy.wait_send()


def deliver(*refs):
    copies = [
        pltpu.make_async_copy(refs[i], refs[4 + i], refs[8].at[i]) for i in range(4)
    ]
    for copy in copies:
        copy.start()
    for copy in copies:
        copy.wait()


def local(n_pat, n_feat, visits, counts, weight, core, factor, static_data, static_factor):
    rows, features = visits.shape
    patients, rank = weight.shape
    columns = static_data.shape[1]
    chunks = 16
    tiles = max(features // 512, 1)
    core_rows = max(rank // n_pat, 16)
    owners = rank // core_rows
    piece = features // n_pat
    blocks = rows // BLK
    vmem, dma = pltpu.VMEM, pltpu.SemaphoreType.DMA
    scratch = [
        vmem((patients, rank), F32),
        vmem((rank, rank), F32),
        vmem((features, rank), BF16),
        vmem((patients, columns), BF16),
        vmem((columns, rank), BF16),
        dma((5,)),
        vmem((rows, features), BF16),
        vmem((rows, rank), F32),
        vmem((rows, rank), F32),
        vmem((4, rows, rank), jnp.int16),
        vmem((4, chunks, blocks // chunks, rank), F32),
        vmem((2, owners, core_rows, rank), F32),
        vmem((n_feat, 2, core_rows, rank), F32),
        vmem((2, core_rows, rank), F32),
        vmem((n_pat, 2, core_rows, rank), F32),
        vmem((patients, rank), F32),
        vmem((n_feat, patients, rank), F32),
        vmem((n_pat, patients, rank), F32),
        vmem((n_pat, patients, columns), F32),
        vmem((4, rank, rank), F32),
        vmem((rank, rank), F32),
        vmem((4, rank, rank), F32),
        vmem((rows, rank), F32),
        vmem((rows, rank), F32),
        vmem((blocks, rank, rank), F32),
        vmem((patients, rank, rank), F32),
        vmem((patients, rank, rank), F32),
        vmem((patients, rank, rank), F32),
        vmem((patients, 2 * rank, 2 * rank), BF16),
        vmem((rank, rows), BF16),
        vmem((rank, 6 * rank), BF16),
        vmem((patients, rank), F32),
        vmem((patients, rank), F32),
        vmem((owners, core_rows, rank), F32),
        vmem((owners, core_rows, rank), F32),
        vmem((n_pat, piece, rank), BF16),
        vmem((n_pat, piece, rank), BF16),
        vmem((n_pat, core_rows, rank), F32),
        vmem((piece, rank), BF16),
        vmem((n_pat, piece, rank), BF16),
        vmem((core_rows, rank), F32),
        vmem((n_pat, core_rows, rank), F32),
        dma((chunks,)),
        dma((2, 2, chunks)),
        dma((2, 2, chunks)),
    ]
    scratch += [dma((n_feat,))] * 8 + [dma((4,))] * 2 + [dma((n_pat,))] * 14
    anywhere = pl.BlockSpec(memory_space=pl.ANY)
    near_by = pl.BlockSpec(memory_space=pltpu.VMEM)
    shapes = ((rank, rank), (features, rank), (patients, rank), (columns, rank))
    results = pl.pallas_call(
        functools.partial(kernel, n_pat, n_feat, chunks, tiles),
        out_shape=tuple(vmem(shape, F32) for shape in shapes),
        in_specs=[pl.BlockSpec(memory_space=pltpu.SMEM)] + [anywhere] * 6,
        out_specs=(near_by,) * 4,
        scratch_shapes=scratch,
        compiler_params=pltpu.CompilerParams(
            collective_id=0, has_side_effects=True, vmem_limit_bytes=56 * 1024 * 1024
        ),
        name="sweep",
    )(counts, visits, weight, core, factor, static_data, static_factor)
    results = [pltpu.with_memory_space_constraint(x, pltpu.VMEM) for x in results]
    return pl.pallas_call(
        deliver,
        out_shape=tuple(jax.ShapeDtypeStruct(shape, F32) for shape in shapes),
        in_specs=[near_by] * 4,
        out_specs=(anywhere,) * 4,
        scratch_shapes=[dma((4,))],
        name="deliver",
    )(*results)


def solution(mesh):
    return jax.shard_map(
        functools.partial(local, mesh.shape["pat"], mesh.shape["feat"]),
        mesh=mesh,
        in_specs=(
            P("pat", "feat"),
            P("pat"),
            P("pat", None),
            P(),
            P("feat", None),
            P("pat", "feat"),
            P("feat", None),
        ),
        out_specs=(P(), P("feat", None), P("pat", None), P("feat", None)),
        check_vma=False,
    )
```

```python
import functools

import jax
import jax.numpy as jnp
from jax import lax
from jax.experimental import pallas as pl
from jax.experimental.pallas import tpu as pltpu
from jax.sharding import PartitionSpec as P

BLK = 128
NS_STEPS = 8
MU_RIDGE = 1.0
MAXV = 512
LEVELS = 32766.0
F32 = jnp.float32
BF16 = jnp.bfloat16
MESH = pl.DeviceIdType.MESH

NN = (((1,), (0,)), ((), ()))
NT = (((1,), (1,)), ((), ()))
TN = (((0,), (0,)), ((), ()))


def dg(a, b, dims):
    return lax.dot_general(a, b, dims, preferred_element_type=F32)


def split(x):
    hi = x.astype(BF16)
    return hi, (x - hi.astype(F32)).astype(BF16)


def join(x):
    return jnp.concatenate(split(x), axis=1)


def twice(x):
    wide = join(x)
    return jnp.concatenate([wide, wide], axis=0)


def halves_sum(x):
    n = x.shape[1] // 2
    return x[:, :n] + x[:, n:]


def dot4(a, b):
    return halves_sum(dg(join(a), twice(b), NN))


def dot4_nt(a, b):
    hi, lo = split(b)
    rows = jnp.concatenate(
        [jnp.concatenate([hi, hi], axis=1), jnp.concatenate([lo, lo], axis=1)], axis=0
    )
    return halves_sum(dg(join(a), rows, NT))


def dot4_tn(a, b):
    return halves_sum(dg(jnp.concatenate(split(a), axis=0), twice(b), TN))


def thirds(x):
    high = x.astype(BF16)
    rest = x - high.astype(F32)
    middle = rest.astype(BF16)
    return high, middle, (rest - middle.astype(F32)).astype(BF16)


def exact(a, b, dims=NN):
    return lax.dot_general(
        a, b, dims, precision=lax.Precision.HIGHEST, preferred_element_type=F32
    )


def solve(rhs, matrix, inverse):
    guess = dot4(rhs, inverse)
    return guess + dot4(rhs - exact(guess, matrix), inverse)


def kernel(
    n_pat, n_feat, chunks, tiles,
    counts, visits, weight_hbm, core_hbm, factor_hbm, data_hbm, static_hbm,
    core_new, feature_new, patient_new, static_new,
    weight, core, factor_in, static_data, static_factor, input_sem,
    vis, proj, total, codes, scales,
    gram_own, gram_parts, gram_mine, gram_all, coupled_own, coupled_parts,
    weights_all, static_all,
    mats, work, inverses, wides, row_weights, squares, grams, factors, halves, mappers, updates, left,
    patient_sum, patient_used, core_sum_own, core_used,
    terms_out, terms_in, core_in, new_out, new_in, coreg_out, coreg_in,
    vis_sem, line_send, line_recv,
    gram_send, gram_recv, coupled_send, coupled_recv, patient_send, patient_recv,
    core_z_send, core_z_recv, inv_send, inv_recv,
    gram_all_send, gram_all_recv, weight_send, weight_recv, static_send, static_recv,
    terms_send, terms_recv, core_send, core_recv,
    new_send, new_recv, coreg_send, coreg_recv, pass_send,
):
    me = lax.axis_index("pat")
    z = lax.axis_index("feat")
    rank = core.shape[0]
    rows = visits.shape[0]
    rows_chunk = rows // chunks
    patients = weight.shape[0]
    features = visits.shape[1]
    piece = features // n_pat
    core_rows = coreg_out.shape[0]
    owners = rank // core_rows
    blocks = rows // BLK
    per_chunk = rows_chunk // BLK
    inner = z > 0
    outer = z < n_feat - 1
    lower = z < n_feat // 2
    source = n_feat // 2
    quad = 4

    def remote(src, dst, send, recv, **where):
        return pltpu.make_async_remote_copy(
            src_ref=src, dst_ref=dst, send_sem=send, recv_sem=recv,
            device_id=where, device_id_type=MESH,
        )

    def span(c):
        return pl.ds(pl.multiple_of(c * rows_chunk, rows_chunk), rows_chunk)

    def load(c):
        return pltpu.make_async_copy(visits.at[span(c)], vis.at[span(c)], vis_sem.at[c])

    def pat_peer(d):
        return lax.rem(me + d, n_pat)

    def feat_peer(d):
        return lax.rem(z + d, n_feat)

    inputs = [
        pltpu.make_async_copy(source_ref, held, input_sem.at[i])
        for i, (source_ref, held) in enumerate(
            (
                (factor_hbm, factor_in), (static_hbm, static_factor), (data_hbm, static_data),
                (weight_hbm, weight), (core_hbm, core),
            )
        )
    ]
    for copy in inputs:
        copy.start()

    @pl.loop(0, chunks)
    def _(c):
        load(c).start()

    barrier = pltpu.get_barrier_semaphore()
    for d in range(1, n_pat):
        pl.semaphore_signal(
            barrier, inc=1, device_id={"pat": pat_peer(d)}, device_id_type=MESH
        )
    for d in range(1, n_feat):
        pl.semaphore_signal(
            barrier, inc=1, device_id={"feat": feat_peer(d)}, device_id_type=MESH
        )

    for copy in inputs:
        copy.wait()
    weights_all[me] = weight[...]
    static_all[me] = static_data[...].astype(F32)
    gram_own[0] = dg(factor_in[...], factor_in[...], TN).reshape(owners, core_rows, rank)
    gram_own[1] = dg(static_factor[...], static_factor[...], TN).reshape(owners, core_rows, rank)
    coupled_own[...] = dg(static_data[...], static_factor[...], NN)
    mine = lax.rem(me, owners)
    for m in range(2):
        gram_parts[z, m] = gram_own[m, mine]
    coupled_parts[z] = coupled_own[...]

    pl.semaphore_wait(barrier, n_pat - 1 + n_feat - 1)

    def gram_copy(d):
        return remote(
            gram_parts.at[z], gram_parts.at[z], gram_send.at[d], gram_recv.at[z], feat=feat_peer(d)
        )

    def coupled_copy(d):
        return remote(
            coupled_own, coupled_parts.at[z], coupled_send.at[d], coupled_recv.at[z],
            feat=feat_peer(d),
        )

    def weight_copy(d):
        return remote(
            weights_all.at[me], weights_all.at[me], weight_send.at[d], weight_recv.at[me],
            pat=pat_peer(d),
        )

    def static_copy(d):
        return remote(
            static_all.at[me], static_all.at[me], static_send.at[d], static_recv.at[me],
            pat=pat_peer(d),
        )

    def gram_all_copy(d):
        return remote(
            gram_mine, gram_all.at[me], gram_all_send.at[d], gram_all_recv.at[me], pat=pat_peer(d)
        )

    for d in range(1, n_feat):
        gram_copy(d).start()
        coupled_copy(d).start()
    for d in range(1, n_pat):
        weight_copy(d).start()
        static_copy(d).start()

    def each_peer(fn):
        for d in range(1, n_pat):
            fn(d, pat_peer(d))

    def arrived(buffer, send, recv):
        def one(d, peer):
            remote(
                buffer.at[peer], buffer.at[peer], send.at[d], recv.at[peer], pat=peer
            ).wait_recv()

        each_peer(one)

    def arrived_z(buffer, send, recv):
        for d in range(1, n_feat):
            peer = feat_peer(d)
            remote(
                buffer.at[peer], buffer.at[peer], send.at[d], recv.at[peer], feat=peer
            ).wait_recv()

    UP_OUT, DOWN_OUT, LOW, HIGH = 0, 1, 2, 3

    def line_copies(c, up):
        way = 0 if up else 1
        out, into = (UP_OUT, LOW) if up else (DOWN_OUT, HIGH)
        peer = z + 1 if up else z - 1
        return (
            remote(
                codes.at[out, span(c)], codes.at[into, span(c)],
                line_send.at[way, 0, c], line_recv.at[way, 0, c], feat=peer,
            ),
            remote(
                scales.at[out, c], scales.at[into, c],
                line_send.at[way, 1, c], line_recv.at[way, 1, c], feat=peer,
            ),
        )

    def block_span(c, b):
        return pl.ds(pl.multiple_of(c * rows_chunk + b * BLK, BLK), BLK)

    def decode(slot, c, b):
        return codes[slot, block_span(c, b), :].astype(jnp.int32).astype(F32) * scales[
            slot, c, pl.ds(b, 1), :
        ]

    def post(c, up, values):
        slot = UP_OUT if up else DOWN_OUT
        for b in range(per_chunk):
            value = values(b)
            top = jnp.maximum(jnp.max(jnp.abs(value), axis=0, keepdims=True), 1e-30)
            code = jnp.round(value * (LEVELS / top)).astype(jnp.int32)
            codes[slot, block_span(c, b), :] = code.astype(jnp.int16)
            scales[slot, c, pl.ds(b, 1), :] = top * (1.0 / LEVELS)
        for copy in line_copies(c, up):
            copy.start()

    def relay(c, up):
        slot = LOW if up else HIGH
        for copy in line_copies(c, up):
            copy.wait_recv()

        @pl.when(outer if up else inner)
        def _():
            post(c, up, lambda b: proj[block_span(c, b), :] + decode(slot, c, b))

    def near(c):
        @pl.when(inner & lower)
        def _():
            relay(c, True)

        @pl.when(outer & jnp.logical_not(lower))
        def _():
            relay(c, False)

    def far(c):
        @pl.when(lower)
        def _():
            relay(c, False)

        @pl.when(jnp.logical_not(lower))
        def _():
            relay(c, True)

    def project(first, last):
        @pl.loop(first // 2, last // 2)
        def _(p):
            load(2 * p).wait()
            load(2 * p + 1).wait()
            both = pl.ds(pl.multiple_of(p * 2 * rows_chunk, rows_chunk), 2 * rows_chunk)
            proj[both, :] = dg(vis[both, :], factor_in[...], NN)

            @pl.when(z == 0)
            def _():
                for i in range(2):
                    post(2 * p + i, True, lambda b, i=i: proj[block_span(2 * p + i, b), :])

            @pl.when(z == n_feat - 1)
            def _():
                for i in range(2):
                    post(2 * p + i, False, lambda b, i=i: proj[block_span(2 * p + i, b), :])

    lane = lax.broadcasted_iota(jnp.int32, (rank, rank), 1)
    sub = lax.broadcasted_iota(jnp.int32, (rank, rank), 0)
    identity = (lane == sub).astype(F32)
    lane_row = lax.broadcasted_iota(jnp.int32, (1, rank), 1)
    sub_col = lax.broadcasted_iota(jnp.int32, (rank, 1), 0)

    def eliminate(k):
        n = k + 1
        whole = work[...]
        row_a = work[pl.ds(k, 1), :]
        row_b = work[pl.ds(n, 1), :]

        def pick(row, at):
            return jnp.sum(jnp.where(lane_row == at, row, 0.0), axis=1, keepdims=True)

        aa, ab, ba, bb = pick(row_a, k), pick(row_a, n), pick(row_b, k), pick(row_b, n)
        column_a = jnp.sum(jnp.where(lane == k, whole, 0.0), axis=1, keepdims=True)
        column_b = jnp.sum(jnp.where(lane == n, whole, 0.0), axis=1, keepdims=True)
        inverse = 1.0 / (aa * bb - ab * ba)
        row_a = jnp.where(lane_row == k, 1.0, jnp.where(lane_row == n, 0.0, row_a))
        row_b = jnp.where(lane_row == n, 1.0, jnp.where(lane_row == k, 0.0, row_b))
        scaled_a = (bb * inverse) * row_a - (ab * inverse) * row_b
        scaled_b = (aa * inverse) * row_b - (ba * inverse) * row_a
        pivots = (lane == k) | (sub == k) | (lane == n) | (sub == n)
        cleared = jnp.where(pivots, 0.0, whole)
        column_a = jnp.where(sub_col == k, -1.0, jnp.where(sub_col == n, 0.0, column_a))
        column_b = jnp.where(sub_col == n, -1.0, jnp.where(sub_col == k, 0.0, column_b))
        work[...] = cleared - column_a * scaled_a - column_b * scaled_b

    starts, ends, lives = [], [], []
    position = jnp.int32(0)
    for k in range(patients):
        starts.append(position)
        lives.append(position + counts[k])
        position = position + ((counts[k] + (BLK - 1)) & (-BLK))
        ends.append(position)

    start_row = jnp.full((1, rank), rows, jnp.int32)
    live_row = jnp.zeros((1, rank), jnp.int32)
    patient_col = lax.broadcasted_iota(jnp.int32, (patients, 1), 0)
    start_col = jnp.full((patients, 1), rows, jnp.int32)
    end_col = jnp.zeros((patients, 1), jnp.int32)
    for k in range(patients):
        start_row = jnp.where(lane_row == k, starts[k], start_row)
        live_row = jnp.where(lane_row == k, lives[k], live_row)
        start_col = jnp.where(patient_col == k, starts[k], start_col)
        end_col = jnp.where(patient_col == k, ends[k], end_col)
    weight_pair = join(
        jnp.concatenate([weight[...], jnp.zeros((rank - patients, rank), F32)], axis=0)
    )
    chunk_row = lax.broadcasted_iota(jnp.int32, (rows_chunk, rank), 0)

    def finish(c):
        total[span(c), :] = proj[span(c), :]

        @pl.when(inner)
        def _():
            for b in range(per_chunk):
                total[block_span(c, b), :] += decode(LOW, c, b)

        @pl.when(outer)
        def _():
            for b in range(per_chunk):
                total[block_span(c, b), :] += decode(HIGH, c, b)

        at = chunk_row + c * rows_chunk
        live = jnp.where((at >= start_row) & (at < live_row), 1.0, 0.0).astype(BF16)
        by_row = halves_sum(dg(live, weight_pair, NN))
        wide = total[span(c), :] * by_row
        row_weights[span(c), :] = by_row
        wides[span(c), :] = wide
        for b in range(per_chunk):
            one = join(wide[b * BLK : (b + 1) * BLK])
            both = dg(one, one, TN)
            squares[c * per_chunk + b] = halves_sum(both[:rank] + both[rank:])

    lag = 2
    early = 3
    pairs = rank // 2
    steps = chunks - lag - early - 1
    share = pairs // steps

    def eliminate_some(first, count):
        @pl.loop(0, count)
        def _(j):
            eliminate(2 * (first + j))

    project(0, 10)
    near(0)
    project(10, 12)
    arrived_z(gram_parts, gram_send, gram_recv)
    gram_mine[...] = jnp.sum(gram_parts[...], axis=0)
    gram_all[me] = gram_mine[...]
    for d in range(1, n_pat):
        gram_all_copy(d).start()
    project(12, 14)
    near(1)
    project(14, chunks)

    @pl.loop(lag, lag + early)
    def _(c):
        near(c)
        far(c - lag)
        finish(c - lag)

    arrived(weights_all, weight_send, weight_recv)
    arrived(gram_all, gram_all_send, gram_all_recv)

    all_rows = weights_all[...].reshape(n_pat * patients, rank)
    weight_gram = exact(all_rows, all_rows, TN)
    core_gram = exact(core[...], core[...], TN)
    feature_gram = jnp.concatenate([gram_all[q, 0] for q in range(owners)], axis=0)
    static_gram = jnp.concatenate([gram_all[q, 1] for q in range(owners)], axis=0)
    mats[0] = feature_gram * weight_gram + MU_RIDGE * identity
    mats[1] = core_gram * weight_gram + MU_RIDGE * identity
    mats[2] = core_gram * feature_gram + static_gram + MU_RIDGE * identity
    mats[3] = weight_gram + MU_RIDGE * identity
    which = lax.rem(me, quad)
    work[...] = mats[which]

    @pl.loop(lag + early, chunks - 1)
    def _(c):
        near(c)
        far(c - lag)
        finish(c - lag)
        eliminate_some((c - lag - early) * share, share)

    near(chunks - 1)
    far(chunks - 1 - lag)
    finish(chunks - 1 - lag)
    eliminate_some(steps * share, pairs - steps * share)

    @pl.loop(chunks, chunks + lag)
    def _(c):
        far(c - lag)
        finish(c - lag)

    def inv_peer(d):
        return lax.div(me, quad) * quad + lax.rem(me + d, quad)

    inverses[which] = work[...]

    def inv_copy(d):
        return remote(
            inverses.at[which], inverses.at[which], inv_send.at[d], inv_recv.at[which],
            pat=inv_peer(d),
        )

    for d in range(1, quad):
        inv_copy(d).start()

    most = MAXV // BLK
    every = range(patients)
    sums = []
    for k in every:
        first = lax.shift_right_logical(starts[k], 7)
        after = lax.shift_right_logical(ends[k], 7)
        square = squares[first]
        for i in range(1, most):
            keep = jnp.where(first + i < after, 1.0, 0.0).astype(F32)
            square = square + keep * squares[jnp.minimum(first + i, blocks - 1)]
        sums.append(square)
    sums = [dot4(core[...], square) for square in sums]
    for k in every:
        halves[k] = sums[k]
    products = [dot4_nt(half, core[...]) for half in sums]
    for k in every:
        trace = jnp.sum(
            jnp.sum(products[k] * identity, axis=1, keepdims=True), axis=0, keepdims=True
        )
        grams[k] = products[k] / trace
        factors[k] = identity / jnp.sqrt(trace)

    def corrections():
        return [twice(1.5 * identity - 0.5 * grams[k]) for k in every]

    @pl.loop(0, NS_STEPS - 1)
    def _(step):
        rights, firsts = [], []
        for k in every:
            moment = grams[k]
            right = twice(1.5 * identity - 0.5 * moment)
            both = jnp.concatenate([factors[k], moment], axis=0)
            rights.append(right)
            firsts.append(dg(join(both), right, NN))
        for k in every:
            both = halves_sum(firsts[k])
            factors[k] = both[:rank]
            grams[k] = halves_sum(dg(join(both[rank:]), rights[k], NN))

    rights = corrections()
    lasts = [halves_sum(dg(join(factors[k]), rights[k], NN)) for k in every]
    mapped_core = [dot4(factor, core[...]) for factor in lasts]
    for k in every:
        mappers[k] = twice(dot4_tn(core[...], mapped_core[k]))
    parts = [dot4_tn(lasts[k], halves[k]) for k in every]
    core_terms = parts[0]
    for k in range(1, patients):
        core_terms = core_terms + parts[k]

    core_sum_own[...] = core_terms.reshape(owners, core_rows, rank)

    def core_z_copy(d):
        return remote(
            core_sum_own, core_used, core_z_send.at[d], core_z_recv.at[0], feat=feat_peer(d)
        )

    def patient_copy(d):
        return remote(
            patient_sum, patient_used, patient_send.at[d], patient_recv.at[0], feat=feat_peer(d)
        )

    @pl.when(z == source)
    def _():
        core_used[...] = core_sum_own[...]
        for d in range(1, n_feat):
            core_z_copy(d).start()

    group = 8

    def map_group(g, sums):
        raw = []
        for i in range(group):
            at = (g * group + i) * BLK
            owner = jnp.int32(0)
            for k in range(patients - 1):
                owner = owner + jnp.where(at >= ends[k], 1, 0)
            wide = wides[pl.ds(pl.multiple_of(at, BLK), BLK), :]
            raw.append(dg(join(wide), mappers[owner], NN))
        for i in range(group):
            at = (g * group + i) * BLK
            span_b = pl.ds(pl.multiple_of(at, BLK), BLK)
            mapped = halves_sum(raw[i])
            products = mapped * total[span_b, :]
            updates[:, span_b] = jnp.transpose(mapped * row_weights[span_b, :]).astype(BF16)
            member = jnp.where((at >= start_col) & (at < end_col), 1.0, 0.0).astype(F32)
            sums = sums + member * jnp.sum(products, axis=0, keepdims=True)
        return sums

    patient_sum[...] = lax.fori_loop(
        0, blocks // group, map_group, jnp.zeros((patients, rank), F32)
    )

    @pl.when(z == source)
    def _():
        patient_used[...] = patient_sum[...]
        for d in range(1, n_feat):
            patient_copy(d).start()

    for d in range(1, quad):
        peer = inv_peer(d)
        slot = lax.rem(me + d, quad)
        remote(
            inverses.at[slot], inverses.at[slot], inv_send.at[d], inv_recv.at[slot], pat=peer
        ).wait_recv()

    width = features // tiles
    per = n_pat // tiles

    def terms_copy(peer):
        return remote(
            terms_out.at[peer], terms_in.at[me], terms_send.at[peer], terms_recv.at[me], pat=peer
        )

    def core_copy(d):
        peer = pat_peer(d)
        return remote(
            core_used.at[lax.rem(peer, owners)], core_in.at[me], core_send.at[d],
            core_recv.at[me], pat=peer,
        )

    def some_tiles(first, last):
        @pl.loop(first, last)
        def _(s):
            tile = lax.rem(lax.div(me, per) + 1 + s, tiles)
            columns = pl.ds(pl.multiple_of(tile * width, width), width)
            high, middle, low = thirds(dg(updates[...], vis[:, columns], NN))
            right = jnp.concatenate([high, high, middle, middle, low, high], axis=0)
            acc = jnp.transpose(dg(left[...], right, NN)).astype(BF16)
            for j in range(per):
                peer = tile * per + j
                terms_out[peer] = acc[j * piece : (j + 1) * piece]

                @pl.when(peer != me)
                def _():
                    terms_copy(peer).start()

    high, middle, low = thirds(inverses[1])
    left[...] = jnp.concatenate([high, middle, high, middle, high, low], axis=1)

    some_tiles(0, tiles // 2)

    @pl.when(z != source)
    def _():
        core_z_copy(0).wait_recv()

    core_in[me] = core_used[mine]
    for d in range(1, n_pat):
        core_copy(d).start()

    some_tiles(tiles // 2, tiles)

    @pl.when(z != source)
    def _():
        patient_copy(0).wait_recv()

    arrived_z(coupled_parts, coupled_send, coupled_recv)
    coupled = jnp.sum(coupled_parts[...], axis=0)
    patient_new[...] = solve(patient_used[...] + coupled, mats[2], inverses[2])
    arrived(static_all, static_send, static_recv)
    static_terms = exact(static_all[...].reshape(n_pat * patients, -1), all_rows, TN)
    static_new[...] = solve(static_terms, mats[3], inverses[3])

    arrived(core_in, core_send, core_recv)
    terms_in[me] = terms_out[me]
    arrived(terms_in, terms_send, terms_recv)

    core_sum = jnp.sum(core_in[...], axis=0)
    coreg_out[...] = solve(core_sum, mats[0], inverses[0])
    terms_sum = jnp.sum(terms_in[...].astype(F32), axis=0)
    new_out[...] = terms_sum.astype(BF16)

    partner = me + 1 - 2 * lax.rem(me, 2)

    def same_core(j):
        return lax.rem(me + 2 * j, n_pat)

    def new_copy(j):
        return remote(
            new_out, new_in.at[me], new_send.at[j], new_recv.at[me],
            pat=same_core(j) if j else partner,
        )

    def pass_copy(j):
        held = same_core(j)
        return remote(
            new_in.at[held], new_in.at[held], pass_send.at[j], new_recv.at[held], pat=partner
        )

    def coreg_copy(d):
        return remote(
            coreg_out, coreg_in.at[me], coreg_send.at[d], coreg_recv.at[me], pat=pat_peer(d)
        )

    for j in range(1, n_pat // 2):
        new_copy(j).start()
    new_copy(0).start()
    for d in range(1, n_pat):
        coreg_copy(d).start()
    new_in[me] = new_out[...]
    coreg_in[me] = coreg_out[...]

    def landed(held):
        remote(
            new_in.at[held], new_in.at[held], pass_send.at[0], new_recv.at[held], pat=partner
        ).wait_recv()

    for j in range(1, n_pat // 2):
        landed(same_core(j))
        pass_copy(j).start()
    arrived(coreg_in, coreg_send, coreg_recv)
    for q in range(owners):
        core_new[pl.ds(q * core_rows, core_rows), :] = coreg_in[q]
    landed(partner)
    for j in range(1, n_pat // 2):
        landed(lax.rem(partner + 2 * j, n_pat))
    feature_new[...] = new_in[...].astype(F32).reshape(features, rank)

    for d in range(1, n_pat):
        weight_copy(d).wait_send()
        static_copy(d).wait_send()
        gram_all_copy(d).wait_send()
        core_copy(d).wait_send()
        coreg_copy(d).wait_send()
        terms_copy(pat_peer(d)).wait_send()
    for d in range(1, quad):
        inv_copy(d).wait_send()
    for j in range(n_pat // 2):
        new_copy(j).wait_send()
    for j in range(1, n_pat // 2):
        pass_copy(j).wait_send()
    for d in range(1, n_feat):
        gram_copy(d).wait_send()
        coupled_copy(d).wait_send()

    @pl.when(z == source)
    def _():
        for d in range(1, n_feat):
            core_z_copy(d).wait_send()
            patient_copy(d).wait_send()

    @pl.loop(0, chunks)
    def _(c):
        @pl.when(outer)
        def _():
            for copy in line_copies(c, True):
                copy.wait_send()

        @pl.when(inner)
        def _():
            for copy in line_copies(c, False):
                copy.wait_send()


def deliver(*refs):
    copies = [
        pltpu.make_async_copy(refs[i], refs[4 + i], refs[8].at[i]) for i in range(4)
    ]
    for copy in copies:
        copy.start()
    for copy in copies:
        copy.wait()


def local(n_pat, n_feat, visits, counts, weight, core, factor, static_data, static_factor):
    rows, features = visits.shape
    patients, rank = weight.shape
    columns = static_data.shape[1]
    chunks = 16
    tiles = max(features // 512, 1)
    core_rows = max(rank // n_pat, 16)
    owners = rank // core_rows
    piece = features // n_pat
    blocks = rows // BLK
    vmem, dma = pltpu.VMEM, pltpu.SemaphoreType.DMA
    scratch = [
        vmem((patients, rank), F32),
        vmem((rank, rank), F32),
        vmem((features, rank), BF16),
        vmem((patients, columns), BF16),
        vmem((columns, rank), BF16),
        dma((5,)),
        vmem((rows, features), BF16),
        vmem((rows, rank), F32),
        vmem((rows, rank), F32),
        vmem((4, rows, rank), jnp.int16),
        vmem((4, chunks, blocks // chunks, rank), F32),
        vmem((2, owners, core_rows, rank), F32),
        vmem((n_feat, 2, core_rows, rank), F32),
        vmem((2, core_rows, rank), F32),
        vmem((n_pat, 2, core_rows, rank), F32),
        vmem((patients, rank), F32),
        vmem((n_feat, patients, rank), F32),
        vmem((n_pat, patients, rank), F32),
        vmem((n_pat, patients, columns), F32),
        vmem((4, rank, rank), F32),
        vmem((rank, rank), F32),
        vmem((4, rank, rank), F32),
        vmem((rows, rank), F32),
        vmem((rows, rank), F32),
        vmem((blocks, rank, rank), F32),
        vmem((patients, rank, rank), F32),
        vmem((patients, rank, rank), F32),
        vmem((patients, rank, rank), F32),
        vmem((patients, 2 * rank, 2 * rank), BF16),
        vmem((rank, rows), BF16),
        vmem((rank, 6 * rank), BF16),
        vmem((patients, rank), F32),
        vmem((patients, rank), F32),
        vmem((owners, core_rows, rank), F32),
        vmem((owners, core_rows, rank), F32),
        vmem((n_pat, piece, rank), BF16),
        vmem((n_pat, piece, rank), BF16),
        vmem((n_pat, core_rows, rank), F32),
        vmem((piece, rank), BF16),
        vmem((n_pat, piece, rank), BF16),
        vmem((core_rows, rank), F32),
        vmem((n_pat, core_rows, rank), F32),
        dma((chunks,)),
        dma((2, 2, chunks)),
        dma((2, 2, chunks)),
    ]
    scratch += [dma((n_feat,))] * 8 + [dma((4,))] * 2 + [dma((n_pat,))] * 15
    anywhere = pl.BlockSpec(memory_space=pl.ANY)
    near_by = pl.BlockSpec(memory_space=pltpu.VMEM)
    shapes = ((rank, rank), (features, rank), (patients, rank), (columns, rank))
    results = pl.pallas_call(
        functools.partial(kernel, n_pat, n_feat, chunks, tiles),
        out_shape=tuple(vmem(shape, F32) for shape in shapes),
        in_specs=[pl.BlockSpec(memory_space=pltpu.SMEM)] + [anywhere] * 6,
        out_specs=(near_by,) * 4,
        scratch_shapes=scratch,
        compiler_params=pltpu.CompilerParams(
            collective_id=0, has_side_effects=True, vmem_limit_bytes=56 * 1024 * 1024
        ),
        name="sweep",
    )(counts, visits, weight, core, factor, static_data, static_factor)
    results = [pltpu.with_memory_space_constraint(x, pltpu.VMEM) for x in results]
    return pl.pallas_call(
        deliver,
        out_shape=tuple(jax.ShapeDtypeStruct(shape, F32) for shape in shapes),
        in_specs=[near_by] * 4,
        out_specs=(anywhere,) * 4,
        scratch_shapes=[dma((4,))],
        name="deliver",
    )(*results)


def solution(mesh):
    return jax.shard_map(
        functools.partial(local, mesh.shape["pat"], mesh.shape["feat"]),
        mesh=mesh,
        in_specs=(
            P("pat", "feat"),
            P("pat"),
            P("pat", None),
            P(),
            P("feat", None),
            P("pat", "feat"),
            P("feat", None),
        ),
        out_specs=(P(), P("feat", None), P("pat", None), P("feat", None)),
        check_vma=False,
    )
```
